256 devices in a mesh: region: 16 (over x, y), period: 16 (over z, core).
Axes of the slice: x: 4, y: 4, z: 8, core: 2. Of those that a mesh axis runs over, the one named last changes fastest.
Arguments:
- load: float32 [16, 32, 16, 2304], P('region', 'period'), may hold values from -6 to 6
- ptdf: bfloat16 [16, 2048, 2304], P('region'), may hold values from -0.125 to 0.125
- ptdf_pattern: int32 [16, 16, 18], P('region'), may hold values 0 or 1
- line_limit: float32 [16, 2048], P('region'), may hold values from 0.3 to 3
- unit_bus: int32 [16, 1024], P('region'), may hold values from 0 to 2303
- store_bus: int32 [16, 128], P('region'), may hold values from 0 to 2303
- tie_block: int32 [16, 4], P('region'), may hold values from 0 to 15, as said below
- cost_quad: float32 [16, 1024], P('region'), may hold values from 0.5 to 2
- cost_lin: float32 [16, 1024], P('region'), may hold values from -1 to 1
- gen_limit: float32 [16, 1024], P('region'), may hold values from 0.5 to 2
- ramp_limit: float32 [16, 1024], P('region'), may hold values from 0.05 to 0.5
- retention: float32 [16, 32, 128], P('region', 'period'), may hold values from 0.3 to 1
- store_cap: float32 [16, 128], P('region'), may hold values from 1 to 4
- gen_start: float32 [16, 32, 16, 1024], P('region', 'period'), may hold values from 0 to 1
- charge_start: float32 [16, 32, 16, 128], P('region', 'period'), may hold values from -1.5 to 1.5
Outputs:
- dispatch: float32 [16, 32, 16, 1024], P('region', 'period')
- storage_charge: float32 [16, 32, 16, 128], P('region', 'period')
- line_price: float32 [16, 32, 16, 2048], P('region', 'period')
- tie_price: float32 [16, 32, 16, 512], P('region', 'period')
- penalty: float32 [], replicated
The draws below stay inside these ranges and needn't reach their ends.
Inputs may be any that keep to these rules, and one draw needn't show every extreme that they name: `tie_block`: the 4 blocks of one region are distinct.
All inputs are finite; a program needn't handle non-finite values. No bound on the sum of `ptdf_pattern` on one device may be relied on, other than what follows from the above.
Results may differ from the reference program's by a relative error of at most 0.0032.
Values sent between devices are 32-bit elements; how exact they have to be, the bound alone decides.
A program may use at most 64 MiB of HBM per device.

```python
import math
import jax
import jax.numpy as jnp
import numpy as np
from jax import lax

SCEN = 16
U = 1024
B = 2304
L = 2048
STORAGE_UNITS = 128
BLK = 128
COLORS = 4
ITERS = 2
REGION_COUNT = 16
PERIOD_TOTAL = 32
N_REGION = 16


def draw_tie_block(key, part):
    block_count = L // BLK

    def choose_blocks(subkey):
        return jax.random.permutation(subkey, block_count)[:COLORS]
    picks = jax.vmap(choose_blocks)(jax.random.split(key, REGION_COUNT))
    spaced = jnp.arange(COLORS) * (block_count - 1) // max(COLORS - 1, 1)
    picks = picks.at[0].set(spaced)
    return picks.astype(jnp.int32)


def draw_retention(key, part):
    failure_rate_key, outage_key, reservoir_key = jax.random.split(key, 3)
    top = 30.0
    lowest = jnp.log(0.2 / PERIOD_TOTAL)
    highest = jnp.log(min(top / PERIOD_TOTAL, 0.5))
    failure_rates = jnp.exp(jax.random.uniform(failure_rate_key, (REGION_COUNT, 1, STORAGE_UNITS), jnp.float32, lowest, highest))
    outage_events = jax.random.bernoulli(outage_key, 0.03, (REGION_COUNT, PERIOD_TOTAL, STORAGE_UNITS))
    reservoir_depth = jax.random.uniform(reservoir_key, (REGION_COUNT, PERIOD_TOTAL, STORAGE_UNITS), jnp.float32, 0.5, 0.8)
    return (jnp.exp(-failure_rates) * jnp.where(outage_events, reservoir_depth, 1.0)).astype(jnp.float32)


def plant(entries, stream_key, low, high):
    place = [jax.random.randint(jax.random.fold_in(stream_key, axis), (), 0, length) for axis, length in enumerate(entries.shape)]
    widest = entries.shape.index(max(entries.shape))
    next_to = place[:widest] + [(place[widest] + 1) % entries.shape[widest]] + place[widest + 1:]
    return entries.at[tuple(place)].set(low).at[tuple(next_to)].set(high)


def level_of(own_key, extent, cuts, smallest, high):
    loudness, own = 1.0, jax.random.fold_in(own_key, 6)
    for position, blocks in cuts:
        draws = jnp.exp(jax.random.uniform(jax.random.fold_in(own, position), (blocks,), jnp.float32, smallest / len(cuts), high / len(cuts)))
        loudness = loudness * jnp.repeat(draws, extent[position] // blocks).reshape([-1 if axis == position else 1 for axis in range(len(extent))])
    return loudness


def noise(rng, shape, scale, limit, cuts=(), kind=jnp.bfloat16):
    gain = level_of(rng, shape, cuts, -0.22, 0.18) if cuts else 1.0
    result = jax.random.normal(rng, shape, jnp.float32) * scale * gain
    return jnp.minimum(jnp.maximum(result, -limit), limit).astype(kind)


def setup_inputs(seed: int = 0) -> dict:
    keys = jax.random.split(jax.random.key(seed), 16)
    return {
        "load": noise(keys[0], (REGION_COUNT, PERIOD_TOTAL, SCEN, B), 1.0, 6.0, ((0, 16), (1, 16)), jnp.float32),
        "ptdf": noise(keys[1], (REGION_COUNT, L, B), B ** -0.5, 0.125, ((0, 16),)),
        "ptdf_pattern": plant((jax.random.randint(keys[2], (REGION_COUNT, L // BLK, B // BLK), 0, 4) < 3).astype(jnp.int32), jax.random.fold_in(keys[2], 1), 0, 1),
        "line_limit": jnp.clip(jnp.exp(math.log(3.0) - 2.3025851 * jax.random.uniform(keys[3], (REGION_COUNT, L), jnp.float32) ** level_of(keys[3], (REGION_COUNT, L), ((0, 16),), -0.2, 0.2)), 0.3, 3.0),
        "unit_bus": plant(jax.random.randint(keys[4], (REGION_COUNT, U), 0, B), jax.random.fold_in(keys[4], 1), 0, B - 1).astype(jnp.int32),
        "store_bus": plant(jax.random.randint(keys[5], (REGION_COUNT, STORAGE_UNITS), 0, B), jax.random.fold_in(keys[5], 1), 0, B - 1).astype(jnp.int32),
        "tie_block": draw_tie_block(jax.random.fold_in(keys[15], 71), 0),
        "cost_quad": jnp.clip(jnp.exp(math.log(2.0) - 1.3862944 * jax.random.uniform(keys[7], (REGION_COUNT, U), jnp.float32) ** level_of(keys[7], (REGION_COUNT, U), ((0, 16),), -0.2, 0.2)), 0.5, 2.0),
        "cost_lin": jnp.clip(jax.random.uniform(keys[8], (REGION_COUNT, U), jnp.float32, -1.0, 1.0) * level_of(keys[8], (REGION_COUNT, U), ((0, 16),), -0.4, 0.0), -1.0, 1.0),
        "gen_limit": jnp.clip(jnp.exp(math.log(2.0) - 1.3862944 * jax.random.uniform(keys[9], (REGION_COUNT, U), jnp.float32) ** level_of(keys[9], (REGION_COUNT, U), ((0, 16),), -0.2, 0.2)), 0.5, 2.0),
        "ramp_limit": jnp.clip(jnp.exp(math.log(0.5) - 2.3025851 * jax.random.uniform(keys[10], (REGION_COUNT, U), jnp.float32) ** level_of(keys[10], (REGION_COUNT, U), ((0, 16),), -0.2, 0.2)), 0.05, 0.5),
        "retention": draw_retention(jax.random.fold_in(keys[15], 71), 0),
        "store_cap": jnp.clip(jnp.exp(math.log(4.0) - 1.3862944 * jax.random.uniform(keys[12], (REGION_COUNT, STORAGE_UNITS), jnp.float32) ** level_of(keys[12], (REGION_COUNT, STORAGE_UNITS), ((0, 16),), -0.2, 0.2)), 1.0, 4.0),
        "gen_start": jnp.clip(1.0 * jax.random.uniform(keys[13], (REGION_COUNT, PERIOD_TOTAL, SCEN, U), jnp.float32) ** level_of(keys[13], (REGION_COUNT, PERIOD_TOTAL, SCEN, U), ((0, 16), (1, 16)), -0.2, 0.2), 0.0, 1.0),
        "charge_start": noise(keys[14], (REGION_COUNT, PERIOD_TOTAL, SCEN, STORAGE_UNITS), 0.3, 1.5, ((0, 16), (1, 16)), jnp.float32),
    }


step_size = 0.05
store_weight = 0.1
rho_start = 1.0
small_eps = 1e-5


def spread_pattern(pattern):
    return jnp.repeat(jnp.repeat(pattern, BLK, axis=1), BLK, axis=2)


def reference(load, ptdf, ptdf_pattern, line_limit, unit_bus, store_bus, tie_block, cost_quad, cost_lin, gen_limit, ramp_limit, retention, store_cap, gen_start, charge_start):
    highest = lax.Precision.HIGHEST
    network = (ptdf * spread_pattern(ptdf_pattern).astype(jnp.bfloat16)).astype(jnp.float32)
    bus_range = jnp.arange(B, dtype=jnp.int32)
    unit_map = (unit_bus[:, :, None] == bus_range).astype(jnp.float32)
    store_map = (store_bus[:, :, None] == bus_range).astype(jnp.float32)
    line_range = jnp.arange(L, dtype=jnp.int32)
    block_range = jnp.arange(BLK, dtype=jnp.int32)
    nbits = N_REGION.bit_length() - 1
    first_period = (jnp.arange(PERIOD_TOTAL) == 0)[None, :, None, None]
    flow_cap = line_limit[:, None, None, :]
    ramp_cap = ramp_limit[:, None, None, :]
    capacity = store_cap[:, None, None, :]
    keep_rate = jnp.moveaxis(retention, 1, 0)[:, :, None, :]
    gen = gen_start
    charge = charge_start
    line_dual = jnp.zeros((N_REGION, PERIOD_TOTAL, SCEN, L), jnp.float32)
    tie_dual = [jnp.zeros((N_REGION, PERIOD_TOTAL, SCEN, BLK), jnp.float32) for colour in range(COLORS)]
    ramp_dual = jnp.zeros_like(gen)
    store_dual = jnp.zeros_like(charge)
    balance_dual = jnp.zeros((N_REGION, PERIOD_TOTAL, SCEN), jnp.float32)
    rho = jnp.float32(rho_start)
    zero_level = jnp.zeros((N_REGION, SCEN, STORAGE_UNITS), jnp.float32)
    for iteration in range(ITERS):
        inject = jnp.einsum("rpsu,rub->rpsb", gen, unit_map, precision=highest) - jnp.einsum("rpsk,rkb->rpsb", charge, store_map, precision=highest) - load
        flows = jnp.einsum("rpsb,rlb->rpsl", inject.astype(jnp.bfloat16).astype(jnp.float32), network)
        over = flows - jnp.clip(flows, -flow_cap, flow_cap)
        line_term = line_dual + rho * over
        flow_term = line_term
        primal = jnp.sum(over * over)
        new_ties = []
        for colour in range(COLORS):
            partner = np.arange(N_REGION) ^ (1 << (colour % nbits))
            wanted = tie_block[:, colour][:, None, None] * BLK + block_range[None, None, :]
            picker = (line_range[None, :, None] == wanted).astype(jnp.float32)
            mine = jnp.einsum("rpsl,rlk->rpsk", flows, picker, precision=highest)
            mismatch = mine + mine[partner]
            tie_term = tie_dual[colour] + rho * mismatch
            flow_term = flow_term + jnp.einsum("rpsk,rlk->rpsl", tie_term, picker, precision=highest)
            primal = primal + jnp.sum(mismatch * mismatch)
            new_ties.append(tie_term)
        grad_inject = jnp.einsum("rpsl,rlb->rpsb", flow_term.astype(jnp.bfloat16).astype(jnp.float32), network)
        balance = jnp.mean(inject, axis=3)
        balance_term = balance_dual + rho * balance
        earlier = jnp.concatenate([jnp.zeros_like(gen[:, :1]), gen[:, :-1]], axis=1)
        change = gen - earlier
        ramp_over = change - jnp.clip(change, -ramp_cap, ramp_cap)
        ramp_over = jnp.where(first_period, 0.0, ramp_over)
        ramp_term = ramp_dual + rho * ramp_over
        ramp_later = jnp.concatenate([ramp_term[:, 1:], jnp.zeros_like(ramp_term[:, :1])], axis=1)

        def forward(level, inputs):
            rate, inflow = inputs
            level = rate * level + inflow
            return level, level

        unused, soc = lax.scan(forward, zero_level, (keep_rate, jnp.moveaxis(charge, 1, 0)))
        soc = jnp.moveaxis(soc, 0, 1)
        store_over = soc - jnp.clip(soc, 0.0, capacity)
        store_term = store_dual + rho * store_over

        def backward(carry, inputs):
            rate, term = inputs
            adjoint_now = term + carry
            return rate * adjoint_now, adjoint_now

        unused, adjoint = lax.scan(backward, zero_level, (keep_rate, jnp.moveaxis(store_term, 1, 0)), reverse=True)
        adjoint = jnp.moveaxis(adjoint, 0, 1)
        primal = primal + jnp.sum(ramp_over * ramp_over) + jnp.sum(store_over * store_over) + jnp.sum(balance * balance)
        unit_push = jnp.einsum("rpsb,rub->rpsu", grad_inject, unit_map, precision=highest)
        store_push = jnp.einsum("rpsb,rkb->rpsk", grad_inject, store_map, precision=highest)
        balance_wide = balance_term[..., None]
        grad_gen = cost_quad[:, None, None, :] * gen + cost_lin[:, None, None, :] + unit_push + balance_wide + ramp_term - ramp_later
        grad_charge = store_weight * charge + adjoint - store_push - balance_wide
        gen_next = jnp.clip(gen - step_size * grad_gen, 0.0, gen_limit[:, None, None, :])
        charge_next = jnp.clip(charge - step_size * grad_charge, -0.25 * capacity, 0.25 * capacity)
        gen_step = gen_next - gen
        charge_step = charge_next - charge
        changes = (jnp.sum(gen_step * gen_step) + jnp.sum(charge_step * charge_step)) / (step_size * step_size)
        line_dual = line_term
        tie_dual = new_ties
        ramp_dual = ramp_term
        store_dual = store_term
        balance_dual = balance_term
        rho = rho * ((primal + small_eps) / (changes + small_eps)) ** 0.25
        gen = gen_next
        charge = charge_next
    return gen, charge, line_dual, jnp.concatenate(tie_dual, axis=3), rho
```

```python
import jax
import jax.numpy as jnp
from jax import lax
from jax.sharding import PartitionSpec as P

BLK = 128
COLORS = 4
ITERS = 2


step_size = 0.05
store_weight = 0.1
rho_start = 1.0
small_eps = 1e-05


def swapped(shard, axis, apart):
    return lax.ppermute(shard, axis, [(i, i ^ 1 << apart) for i in range(lax.axis_size(axis))])


def passed_along(value, axis, steps):
    count = lax.axis_size(axis)
    leading, last = (max(0, -steps), min(count, count - steps))
    return lax.ppermute(value, axis, [(source, source + steps) for source in range(leading, last)])


def gathered(shard, axis):
    count, position = (lax.axis_size(axis), lax.axis_index(axis))
    whole, apart = (shard, 1)
    while apart < count:
        other = lax.ppermute(whole, axis, [(i, i ^ apart) for i in range(count)])
        low = position // apart % 2 == 0
        whole = jnp.where(low, jnp.concatenate([whole, other]), jnp.concatenate([other, whole]))
        apart *= 2
    return whole


def total(value, axes):
    for axis in axes:
        count, position = (lax.axis_size(axis), lax.axis_index(axis))
        stride = 1
        while stride < count:
            group = 4 if count % (stride * 4) == 0 else 2
            parts = [value] + [
                lax.ppermute(value, axis, [(i, i ^ j * stride) for i in range(count)])
                for j in range(1, group)
            ]
            stacked = jnp.stack(parts)
            member = position // stride % group
            ordered = [stacked[m ^ member] for m in range(group)]
            while len(ordered) > 1:
                ordered = [ordered[k] + ordered[k + 1] for k in range(0, len(ordered), 2)]
            value = ordered[0]
            stride *= group
    return value


def chain(earlier, later):
    return (earlier[0] * later[0], later[0] * earlier[1] + later[1])


def on_device(
    load,
    ptdf,
    ptdf_pattern,
    line_limit,
    unit_bus,
    store_bus,
    tie_block,
    cost_quad,
    cost_lin,
    gen_limit,
    ramp_limit,
    retention,
    store_cap,
    gen_start,
    charge_start,
):
    highest = lax.Precision.HIGHEST
    demand = load[0]
    periods_here, scenarios, buses = demand.shape
    rows = periods_here * scenarios
    lines = ptdf.shape[1]
    stores = charge_start.shape[3]
    pattern = jnp.repeat(jnp.repeat(ptdf_pattern[0], BLK, axis=0), BLK, axis=1)
    network = ptdf[0] * pattern.astype(jnp.bfloat16)
    bus_range = jnp.arange(buses, dtype=jnp.int32)
    unit_map = (unit_bus[0][:, None] == bus_range[None, :]).astype(jnp.float32)
    store_map = (store_bus[0][:, None] == bus_range[None, :]).astype(jnp.float32)
    flow_cap = line_limit[0][None, :]
    ramp_cap = ramp_limit[0]
    quadratic = cost_quad[0]
    linear_cost = cost_lin[0]
    upper = gen_limit[0]
    capacity = store_cap[0]
    keep_rate = retention[0]
    demand_rows = demand.reshape(rows, buses)
    position = lax.axis_index("period")
    nbits = lax.axis_size("region").bit_length() - 1
    at_start = position == 0
    first_here = position * periods_here
    rate_all = gathered(keep_rate, "period")
    rate_next = jnp.concatenate([rate_all[1:], jnp.ones_like(rate_all[:1])])[:, None, :]
    rate_all = rate_all[:, None, :]
    charge_all = gathered(charge_start[0], "period")
    gen = gen_start[0]
    charge = charge_start[0]
    line_dual = jnp.zeros((rows, lines), jnp.float32)
    tie_dual = [jnp.zeros((rows, BLK), jnp.float32) for colour in range(COLORS)]
    ramp_dual = jnp.zeros_like(gen)
    store_dual = jnp.zeros_like(charge_all)
    balance_dual = jnp.zeros((rows,), jnp.float32)
    rho = jnp.float32(rho_start)
    for iteration in range(ITERS):
        gen_rows = gen.reshape(rows, -1)
        charge_rows = charge.reshape(rows, stores)
        inject = (
            jnp.dot(gen_rows, unit_map, precision=highest)
            - jnp.dot(charge_rows, store_map, precision=highest)
            - demand_rows
        )
        flows = jnp.dot(
            network, inject.astype(jnp.bfloat16).T, preferred_element_type=jnp.float32
        ).T
        over = flows - jnp.clip(flows, -flow_cap, flow_cap)
        line_term = line_dual + rho * over
        flow_term = line_term
        local_primal = jnp.sum(over * over)
        new_ties = []
        for colour in range(COLORS):
            start = tie_block[0, colour] * BLK
            mine = lax.dynamic_slice_in_dim(flows, start, BLK, 1)
            theirs = swapped(mine, "region", colour % nbits)
            mismatch = mine + theirs
            tie_term = tie_dual[colour] + rho * mismatch
            current = lax.dynamic_slice_in_dim(flow_term, start, BLK, 1)
            flow_term = lax.dynamic_update_slice_in_dim(flow_term, current + tie_term, start, 1)
            local_primal = local_primal + jnp.sum(mismatch * mismatch)
            new_ties.append(tie_term)
        grad_inject = jnp.dot(
            flow_term.astype(jnp.bfloat16), network, preferred_element_type=jnp.float32
        )
        balance = jnp.mean(inject, axis=1)
        balance_term = balance_dual + rho * balance
        before = passed_along(gen[-1], "period", 1)
        earlier = jnp.concatenate([before[None], gen[:-1]], axis=0)
        change = gen - earlier
        ramp_over = change - jnp.clip(change, -ramp_cap, ramp_cap)
        ramp_over = jnp.concatenate(
            [jnp.where(at_start, 0.0, ramp_over[:1]), ramp_over[1:]], axis=0
        )
        ramp_term = ramp_dual + rho * ramp_over
        after = passed_along(ramp_term[0], "period", -1)
        ramp_later = jnp.concatenate([ramp_term[1:], after[None]], axis=0)
        unused, soc = lax.associative_scan(
            chain, (jnp.broadcast_to(rate_all, charge_all.shape), charge_all)
        )
        store_over_all = soc - jnp.clip(soc, 0.0, capacity)
        store_term_all = store_dual + rho * store_over_all
        unused, adjoint_all = lax.associative_scan(
            chain,
            (jnp.broadcast_to(rate_next, charge_all.shape), store_term_all),
            reverse=True,
        )
        store_over = lax.dynamic_slice_in_dim(store_over_all, first_here, periods_here, 0)
        adjoint = lax.dynamic_slice_in_dim(adjoint_all, first_here, periods_here, 0)
        local_primal = (
            local_primal
            + jnp.sum(ramp_over * ramp_over)
            + jnp.sum(store_over * store_over)
            + jnp.sum(balance * balance)
        )
        unit_push = jnp.einsum("rb,ub->ru", grad_inject, unit_map, precision=highest).reshape(
            gen.shape
        )
        store_push = jnp.einsum("rb,kb->rk", grad_inject, store_map, precision=highest).reshape(
            charge.shape
        )
        balance_wide = balance_term.reshape(periods_here, scenarios, 1)
        grad_gen = quadratic * gen + linear_cost + unit_push + balance_wide + ramp_term - ramp_later
        grad_charge = store_weight * charge + adjoint - store_push - balance_wide
        gen_next = jnp.clip(gen - step_size * grad_gen, 0.0, upper)
        charge_next = jnp.clip(charge - step_size * grad_charge, -0.25 * capacity, 0.25 * capacity)
        gen_step = gen_next - gen
        charge_step = charge_next - charge
        local_change = (jnp.sum(gen_step * gen_step) + jnp.sum(charge_step * charge_step)) / (
            step_size * step_size
        )
        primal, changes = total(jnp.stack([local_primal, local_change]), ("region", "period"))
        line_dual = line_term
        tie_dual = new_ties
        ramp_dual = ramp_term
        store_dual = store_term_all
        balance_dual = balance_term
        rho = rho * ((primal + small_eps) / (changes + small_eps)) ** 0.25
        gen = gen_next
        charge = charge_next
        if iteration + 1 < ITERS:
            charge_all = gathered(charge, "period")
    tie_out = jnp.concatenate(tie_dual, axis=1).reshape(periods_here, scenarios, COLORS * BLK)
    return (
        gen[None],
        charge[None],
        line_dual.reshape(periods_here, scenarios, lines)[None],
        tie_out[None],
        rho,
    )


def solution(mesh):
    return jax.shard_map(
        on_device,
        mesh=mesh,
        in_specs=(
            P("region", "period", None, None),
            P("region", None, None),
            P("region", None, None),
            P("region", None),
            P("region", None),
            P("region", None),
            P("region", None),
            P("region", None),
            P("region", None),
            P("region", None),
            P("region", None),
            P("region", "period", None),
            P("region", None),
            P("region", "period", None, None),
            P("region", "period", None, None),
        ),
        out_specs=(
            P("region", "period", None, None),
            P("region", "period", None, None),
            P("region", "period", None, None),
            P("region", "period", None, None),
            P(),
        ),
        check_vma=False,
    )
```

```python
import jax
import jax.numpy as jnp
from jax import lax
from jax.experimental import pallas as pl
from jax.experimental.pallas import tpu as pltpu
from jax.sharding import PartitionSpec as P

BLK = 128
COLORS = 4
ITERS = 2
INTERPRET = False


step_size = 0.05
store_weight = 0.1
rho_start = 1.0
small_eps = 1e-05


def swapped(shard, axis, apart):
    return lax.ppermute(shard, axis, [(i, i ^ 1 << apart) for i in range(lax.axis_size(axis))])


def passed_along(value, axis, steps):
    count = lax.axis_size(axis)
    leading, last = (max(0, -steps), min(count, count - steps))
    return lax.ppermute(value, axis, [(source, source + steps) for source in range(leading, last)])


def gathered(shard, axis):
    count, position = (lax.axis_size(axis), lax.axis_index(axis))
    whole, apart = (shard, 1)
    while apart < count:
        other = lax.ppermute(whole, axis, [(i, i ^ apart) for i in range(count)])
        low = position // apart % 2 == 0
        whole = jnp.where(low, jnp.concatenate([whole, other]), jnp.concatenate([other, whole]))
        apart *= 2
    return whole


def total(value, axes):
    for axis in axes:
        count, position = (lax.axis_size(axis), lax.axis_index(axis))
        stride = 1
        while stride < count:
            group = 4 if count % (stride * 4) == 0 else 2
            parts = [value] + [
                lax.ppermute(value, axis, [(i, i ^ j * stride) for i in range(count)])
                for j in range(1, group)
            ]
            stacked = jnp.stack(parts)
            member = position // stride % group
            ordered = [stacked[m ^ member] for m in range(group)]
            while len(ordered) > 1:
                ordered = [ordered[k] + ordered[k + 1] for k in range(0, len(ordered), 2)]
            value = ordered[0]
            stride *= group
    return value


def recurrence(rate, inflow, reverse):
    def advance(level, step):
        level = step[0] * level + step[1]
        return level, level

    start = jnp.zeros(inflow.shape[1:], inflow.dtype)
    return lax.scan(advance, start, (rate, inflow), reverse=reverse, unroll=8)[1]


def masked_transpose_kernel(pattern_ref, factors_ref, out_ref):
    rows = factors_ref.shape[0] // BLK
    first = pl.program_id(0) * rows
    for row in range(rows):
        for col in range(factors_ref.shape[1] // BLK):
            keep = pattern_ref[first + row, col].astype(jnp.float32)
            tile = factors_ref[pl.ds(row * BLK, BLK), pl.ds(col * BLK, BLK)].astype(jnp.float32)
            out_ref[pl.ds(col * BLK, BLK), pl.ds(row * BLK, BLK)] = (tile.T * keep).astype(
                out_ref.dtype
            )


def masked_transpose(pattern, factors):
    lines, buses = factors.shape
    rows = 2 * BLK
    return pl.pallas_call(
        masked_transpose_kernel,
        out_shape=jax.ShapeDtypeStruct((buses, lines), factors.dtype),
        grid_spec=pltpu.PrefetchScalarGridSpec(
            num_scalar_prefetch=1,
            grid=(lines // rows,),
            in_specs=[pl.BlockSpec((rows, buses), lambda i, p: (i, 0))],
            out_specs=pl.BlockSpec((buses, rows), lambda i, p: (0, i)),
        ),
        interpret=INTERPRET,
    )(pattern, factors)


def on_device(
    load,
    ptdf,
    ptdf_pattern,
    line_limit,
    unit_bus,
    store_bus,
    tie_block,
    cost_quad,
    cost_lin,
    gen_limit,
    ramp_limit,
    retention,
    store_cap,
    gen_start,
    charge_start,
):
    highest = lax.Precision.HIGHEST
    demand = load[0]
    periods_here, scenarios, buses = demand.shape
    rows = periods_here * scenarios
    lines = ptdf.shape[1]
    stores = charge_start.shape[3]
    network_t = masked_transpose(ptdf_pattern[0], ptdf[0])
    bus_range = jnp.arange(buses, dtype=jnp.int32)
    unit_map = (unit_bus[0][:, None] == bus_range[None, :]).astype(jnp.float32)
    store_map = (store_bus[0][:, None] == bus_range[None, :]).astype(jnp.float32)
    flow_cap = line_limit[0][None, :]
    ramp_cap = ramp_limit[0]
    quadratic = cost_quad[0]
    linear_cost = cost_lin[0]
    upper = gen_limit[0]
    capacity = store_cap[0]
    keep_rate = retention[0]
    demand_rows = demand.reshape(rows, buses)
    position = lax.axis_index("period")
    nbits = lax.axis_size("region").bit_length() - 1
    at_start = position == 0
    first_here = position * periods_here
    rate_all = gathered(keep_rate, "period")
    rate_next = jnp.concatenate([rate_all[1:], jnp.zeros_like(rate_all[:1])])[:, None, :]
    rate_all = rate_all[:, None, :]
    charge_all = gathered(charge_start[0], "period")
    gen = gen_start[0]
    charge = charge_start[0]
    line_dual = jnp.zeros((rows, lines), jnp.float32)
    tie_dual = [jnp.zeros((rows, BLK), jnp.float32) for colour in range(COLORS)]
    ramp_dual = jnp.zeros_like(gen)
    store_dual = jnp.zeros_like(charge_all)
    balance_dual = jnp.zeros((rows,), jnp.float32)
    rho = jnp.float32(rho_start)
    for iteration in range(ITERS):
        gen_rows = gen.reshape(rows, -1)
        charge_rows = charge.reshape(rows, stores)
        inject = (
            jnp.dot(gen_rows, unit_map, precision=highest)
            - jnp.dot(charge_rows, store_map, precision=highest)
            - demand_rows
        )
        flows = jnp.dot(
            inject.astype(jnp.bfloat16), network_t, preferred_element_type=jnp.float32
        )
        over = flows - jnp.clip(flows, -flow_cap, flow_cap)
        line_term = line_dual + rho * over
        flow_term = line_term
        local_primal = jnp.sum(over * over)
        new_ties = []
        for colour in range(COLORS):
            start = tie_block[0, colour] * BLK
            mine = lax.dynamic_slice_in_dim(flows, start, BLK, 1)
            theirs = swapped(mine, "region", colour % nbits)
            mismatch = mine + theirs
            tie_term = tie_dual[colour] + rho * mismatch
            current = lax.dynamic_slice_in_dim(flow_term, start, BLK, 1)
            flow_term = lax.dynamic_update_slice_in_dim(flow_term, current + tie_term, start, 1)
            local_primal = local_primal + jnp.sum(mismatch * mismatch)
            new_ties.append(tie_term)
        grad_inject = lax.dot_general(
            flow_term.astype(jnp.bfloat16),
            network_t,
            (((1,), (1,)), ((), ())),
            preferred_element_type=jnp.float32,
        )
        balance = jnp.mean(inject, axis=1)
        balance_term = balance_dual + rho * balance
        before = passed_along(gen[-1], "period", 1)
        earlier = jnp.concatenate([before[None], gen[:-1]], axis=0)
        change = gen - earlier
        ramp_over = change - jnp.clip(change, -ramp_cap, ramp_cap)
        ramp_over = jnp.concatenate(
            [jnp.where(at_start, 0.0, ramp_over[:1]), ramp_over[1:]], axis=0
        )
        ramp_term = ramp_dual + rho * ramp_over
        after = passed_along(ramp_term[0], "period", -1)
        ramp_later = jnp.concatenate([ramp_term[1:], after[None]], axis=0)
        soc = recurrence(rate_all, charge_all, False)
        store_over_all = soc - jnp.clip(soc, 0.0, capacity)
        store_term_all = store_dual + rho * store_over_all
        adjoint_all = recurrence(rate_next, store_term_all, True)
        store_over = lax.dynamic_slice_in_dim(store_over_all, first_here, periods_here, 0)
        adjoint = lax.dynamic_slice_in_dim(adjoint_all, first_here, periods_here, 0)
        local_primal = (
            local_primal
            + jnp.sum(ramp_over * ramp_over)
            + jnp.sum(store_over * store_over)
            + jnp.sum(balance * balance)
        )
        unit_push = jnp.einsum("rb,ub->ru", grad_inject, unit_map, precision=highest).reshape(
            gen.shape
        )
        store_push = jnp.einsum("rb,kb->rk", grad_inject, store_map, precision=highest).reshape(
            charge.shape
        )
        balance_wide = balance_term.reshape(periods_here, scenarios, 1)
        grad_gen = quadratic * gen + linear_cost + unit_push + balance_wide + ramp_term - ramp_later
        grad_charge = store_weight * charge + adjoint - store_push - balance_wide
        gen_next = jnp.clip(gen - step_size * grad_gen, 0.0, upper)
        charge_next = jnp.clip(charge - step_size * grad_charge, -0.25 * capacity, 0.25 * capacity)
        gen_step = gen_next - gen
        charge_step = charge_next - charge
        local_change = (jnp.sum(gen_step * gen_step) + jnp.sum(charge_step * charge_step)) / (
            step_size * step_size
        )
        primal, changes = total(jnp.stack([local_primal, local_change]), ("region", "period"))
        line_dual = line_term
        tie_dual = new_ties
        ramp_dual = ramp_term
        store_dual = store_term_all
        balance_dual = balance_term
        rho = rho * ((primal + small_eps) / (changes + small_eps)) ** 0.25
        gen = gen_next
        charge = charge_next
        if iteration + 1 < ITERS:
            charge_all = gathered(charge, "period")
    tie_out = jnp.concatenate(tie_dual, axis=1).reshape(periods_here, scenarios, COLORS * BLK)
    return (
        gen[None],
        charge[None],
        line_dual.reshape(periods_here, scenarios, lines)[None],
        tie_out[None],
        rho,
    )


def solution(mesh):
    return jax.shard_map(
        on_device,
        mesh=mesh,
        in_specs=(
            P("region", "period", None, None),
            P("region", None, None),
            P("region", None, None),
            P("region", None),
            P("region", None),
            P("region", None),
            P("region", None),
            P("region", None),
            P("region", None),
            P("region", None),
            P("region", None),
            P("region", "period", None),
            P("region", None),
            P("region", "period", None, None),
            P("region", "period", None, None),
        ),
        out_specs=(
            P("region", "period", None, None),
            P("region", "period", None, None),
            P("region", "period", None, None),
            P("region", "period", None, None),
            P(),
        ),
        check_vma=False,
    )
```

```python
import jax
import jax.numpy as jnp
from jax import lax
from jax.experimental import pallas as pl
from jax.experimental.pallas import tpu as pltpu
from jax.sharding import PartitionSpec as P

BLK = 128
COLORS = 4
ITERS = 2
INTERPRET = False


step_size = 0.05
store_weight = 0.1
rho_start = 1.0
small_eps = 1e-05


def swapped(shard, axis, apart):
    return lax.ppermute(shard, axis, [(i, i ^ 1 << apart) for i in range(lax.axis_size(axis))])


def passed_along(value, axis, steps):
    count = lax.axis_size(axis)
    leading, last = (max(0, -steps), min(count, count - steps))
    return lax.ppermute(value, axis, [(source, source + steps) for source in range(leading, last)])


def gathered(shard, axis):
    count, position = (lax.axis_size(axis), lax.axis_index(axis))
    whole, apart = (shard, 1)
    while apart < count:
        other = lax.ppermute(whole, axis, [(i, i ^ apart) for i in range(count)])
        low = position // apart % 2 == 0
        whole = jnp.where(low, jnp.concatenate([whole, other]), jnp.concatenate([other, whole]))
        apart *= 2
    return whole


def total(value, axes):
    for axis in axes:
        count, position = (lax.axis_size(axis), lax.axis_index(axis))
        stride = 1
        while stride < count:
            group = 4 if count % (stride * 4) == 0 else 2
            parts = [value] + [
                lax.ppermute(value, axis, [(i, i ^ j * stride) for i in range(count)])
                for j in range(1, group)
            ]
            stacked = jnp.stack(parts)
            member = position // stride % group
            ordered = [stacked[m ^ member] for m in range(group)]
            while len(ordered) > 1:
                ordered = [ordered[k] + ordered[k + 1] for k in range(0, len(ordered), 2)]
            value = ordered[0]
            stride *= group
    return value


def recurrence(rate, inflow, reverse):
    def advance(level, step):
        level = step[0] * level + step[1]
        return level, level

    start = jnp.zeros(inflow.shape[1:], inflow.dtype)
    return lax.scan(advance, start, (rate, inflow), reverse=reverse, unroll=8)[1]


def masked_transpose_kernel(pattern_ref, factors_ref, out_ref):
    rows = factors_ref.shape[0] // BLK
    first = pl.program_id(0) * rows
    for row in range(rows):
        for col in range(factors_ref.shape[1] // BLK):
            keep = pattern_ref[first + row, col].astype(jnp.float32)
            tile = factors_ref[pl.ds(row * BLK, BLK), pl.ds(col * BLK, BLK)].astype(jnp.float32)
            out_ref[pl.ds(col * BLK, BLK), pl.ds(row * BLK, BLK)] = (tile.T * keep).astype(
                out_ref.dtype
            )


def masked_transpose(pattern, factors):
    lines, buses = factors.shape
    rows = 2 * BLK
    return pl.pallas_call(
        masked_transpose_kernel,
        out_shape=jax.ShapeDtypeStruct((buses, lines), factors.dtype),
        grid_spec=pltpu.PrefetchScalarGridSpec(
            num_scalar_prefetch=1,
            grid=(lines // rows,),
            in_specs=[pl.BlockSpec((rows, buses), lambda i, p: (i, 0))],
            out_specs=pl.BlockSpec((buses, rows), lambda i, p: (0, i)),
        ),
        interpret=INTERPRET,
    )(pattern, factors)


def on_device(
    load,
    ptdf,
    ptdf_pattern,
    line_limit,
    unit_bus,
    store_bus,
    tie_block,
    cost_quad,
    cost_lin,
    gen_limit,
    ramp_limit,
    retention,
    store_cap,
    gen_start,
    charge_start,
):
    highest = lax.Precision.HIGHEST
    demand = load[0]
    periods_here, scenarios, buses = demand.shape
    rows = periods_here * scenarios
    lines = ptdf.shape[1]
    stores = charge_start.shape[3]
    network_t = masked_transpose(ptdf_pattern[0], ptdf[0])
    bus_range = jnp.arange(buses, dtype=jnp.int32)
    unit_map = (unit_bus[0][:, None] == bus_range[None, :]).astype(jnp.float32)
    store_map = (store_bus[0][:, None] == bus_range[None, :]).astype(jnp.float32)
    flow_cap = line_limit[0][None, :]
    ramp_cap = ramp_limit[0]
    quadratic = cost_quad[0]
    linear_cost = cost_lin[0]
    upper = gen_limit[0]
    capacity = store_cap[0]
    keep_rate = retention[0]
    demand_rows = demand.reshape(rows, buses)
    position = lax.axis_index("period")
    nbits = lax.axis_size("region").bit_length() - 1
    at_start = position == 0
    at_end = position == lax.axis_size("period") - 1
    first_here = position * periods_here
    rate_all = gathered(keep_rate, "period")
    rate_next = jnp.concatenate([rate_all[1:], jnp.zeros_like(rate_all[:1])])[:, None, :]
    rate_all = rate_all[:, None, :]
    charge_all = gathered(charge_start[0], "period")
    gen = gen_start[0]
    charge = charge_start[0]
    line_dual = jnp.zeros((rows, lines), jnp.float32)
    tie_dual = [jnp.zeros((rows, BLK), jnp.float32) for colour in range(COLORS)]
    ramp_dual = jnp.zeros_like(gen)
    ramp_dual_after = jnp.zeros_like(gen[0])
    store_dual = jnp.zeros_like(charge_all)
    balance_dual = jnp.zeros((rows,), jnp.float32)
    rho = jnp.float32(rho_start)
    for iteration in range(ITERS):
        gen_rows = gen.reshape(rows, -1)
        charge_rows = charge.reshape(rows, stores)
        inject = (
            jnp.dot(gen_rows, unit_map, precision=highest)
            - jnp.dot(charge_rows, store_map, precision=highest)
            - demand_rows
        )
        flows = jnp.dot(
            inject.astype(jnp.bfloat16), network_t, preferred_element_type=jnp.float32
        )
        over = flows - jnp.clip(flows, -flow_cap, flow_cap)
        line_term = line_dual + rho * over
        flow_term = line_term
        local_primal = jnp.sum(over * over)
        new_ties = []
        for colour in range(COLORS):
            start = tie_block[0, colour] * BLK
            mine = lax.dynamic_slice_in_dim(flows, start, BLK, 1)
            theirs = swapped(mine, "region", colour % nbits)
            mismatch = mine + theirs
            tie_term = tie_dual[colour] + rho * mismatch
            current = lax.dynamic_slice_in_dim(flow_term, start, BLK, 1)
            flow_term = lax.dynamic_update_slice_in_dim(flow_term, current + tie_term, start, 1)
            local_primal = local_primal + jnp.sum(mismatch * mismatch)
            new_ties.append(tie_term)
        grad_inject = lax.dot_general(
            flow_term.astype(jnp.bfloat16),
            network_t,
            (((1,), (1,)), ((), ())),
            preferred_element_type=jnp.float32,
        )
        balance = jnp.mean(inject, axis=1)
        balance_term = balance_dual + rho * balance
        before = passed_along(gen[-1], "period", 1)
        following = passed_along(gen[0], "period", -1)
        earlier = jnp.concatenate([before[None], gen[:-1]], axis=0)
        change = gen - earlier
        ramp_over = change - jnp.clip(change, -ramp_cap, ramp_cap)
        ramp_over = jnp.concatenate(
            [jnp.where(at_start, 0.0, ramp_over[:1]), ramp_over[1:]], axis=0
        )
        ramp_term = ramp_dual + rho * ramp_over
        step_after = following - gen[-1]
        after = ramp_dual_after + rho * (step_after - jnp.clip(step_after, -ramp_cap, ramp_cap))
        after = jnp.where(at_end, 0.0, after)
        ramp_later = jnp.concatenate([ramp_term[1:], after[None]], axis=0)
        soc = recurrence(rate_all, charge_all, False)
        store_over_all = soc - jnp.clip(soc, 0.0, capacity)
        store_term_all = store_dual + rho * store_over_all
        adjoint_all = recurrence(rate_next, store_term_all, True)
        store_over = lax.dynamic_slice_in_dim(store_over_all, first_here, periods_here, 0)
        adjoint = lax.dynamic_slice_in_dim(adjoint_all, first_here, periods_here, 0)
        local_primal = (
            local_primal
            + jnp.sum(ramp_over * ramp_over)
            + jnp.sum(store_over * store_over)
            + jnp.sum(balance * balance)
        )
        unit_push = jnp.einsum("rb,ub->ru", grad_inject, unit_map, precision=highest).reshape(
            gen.shape
        )
        store_push = jnp.einsum("rb,kb->rk", grad_inject, store_map, precision=highest).reshape(
            charge.shape
        )
        balance_wide = balance_term.reshape(periods_here, scenarios, 1)
        grad_gen = quadratic * gen + linear_cost + unit_push + balance_wide + ramp_term - ramp_later
        grad_charge = store_weight * charge + adjoint - store_push - balance_wide
        gen_next = jnp.clip(gen - step_size * grad_gen, 0.0, upper)
        charge_next = jnp.clip(charge - step_size * grad_charge, -0.25 * capacity, 0.25 * capacity)
        gen_step = gen_next - gen
        charge_step = charge_next - charge
        local_change = (jnp.sum(gen_step * gen_step) + jnp.sum(charge_step * charge_step)) / (
            step_size * step_size
        )
        partial = jnp.stack([local_primal, local_change])
        if iteration + 1 < ITERS:
            slab = jnp.pad(partial, (0, stores - 2))
            slab = jnp.broadcast_to(slab, (1, scenarios, stores))
            both = gathered(jnp.concatenate([charge_next, slab]), "period")
            both = both.reshape(-1, periods_here + 1, scenarios, stores)
            charge_all = both[:, :periods_here].reshape(-1, scenarios, stores)
            partial = jnp.sum(both[:, periods_here, 0, :2], axis=0)
            primal, changes = total(partial, ("region",))
        else:
            primal, changes = total(partial, ("region", "period"))
        line_dual = line_term
        tie_dual = new_ties
        ramp_dual = ramp_term
        ramp_dual_after = after
        store_dual = store_term_all
        balance_dual = balance_term
        rho = rho * ((primal + small_eps) / (changes + small_eps)) ** 0.25
        gen = gen_next
        charge = charge_next
    tie_out = jnp.concatenate(tie_dual, axis=1).reshape(periods_here, scenarios, COLORS * BLK)
    return (
        gen[None],
        charge[None],
        line_dual.reshape(periods_here, scenarios, lines)[None],
        tie_out[None],
        rho,
    )


def solution(mesh):
    return jax.shard_map(
        on_device,
        mesh=mesh,
        in_specs=(
            P("region", "period", None, None),
            P("region", None, None),
            P("region", None, None),
            P("region", None),
            P("region", None),
            P("region", None),
            P("region", None),
            P("region", None),
            P("region", None),
            P("region", None),
            P("region", None),
            P("region", "period", None),
            P("region", None),
            P("region", "period", None, None),
            P("region", "period", None, None),
        ),
        out_specs=(
            P("region", "period", None, None),
            P("region", "period", None, None),
            P("region", "period", None, None),
            P("region", "period", None, None),
            P(),
        ),
        check_vma=False,
    )
```

```python
import jax
import jax.numpy as jnp
from jax import lax
from jax.experimental import pallas as pl
from jax.experimental.pallas import tpu as pltpu
from jax.sharding import PartitionSpec as P

BLK = 128
COLORS = 4
ITERS = 2
INTERPRET = False


step_size = 0.05
store_weight = 0.1
rho_start = 1.0
small_eps = 1e-05


def swapped(shard, axis, apart):
    return lax.ppermute(shard, axis, [(i, i ^ 1 << apart) for i in range(lax.axis_size(axis))])


def passed_along(value, axis, steps):
    count = lax.axis_size(axis)
    leading, last = (max(0, -steps), min(count, count - steps))
    return lax.ppermute(value, axis, [(source, source + steps) for source in range(leading, last)])


def gathered(shard, axis):
    count, position = (lax.axis_size(axis), lax.axis_index(axis))
    whole, apart = (shard, 1)
    while apart < count:
        other = lax.ppermute(whole, axis, [(i, i ^ apart) for i in range(count)])
        low = position // apart % 2 == 0
        whole = jnp.where(low, jnp.concatenate([whole, other]), jnp.concatenate([other, whole]))
        apart *= 2
    return whole


def total(value, axes):
    for axis in axes:
        count, position = (lax.axis_size(axis), lax.axis_index(axis))
        stride = 1
        while stride < count:
            group = 4 if count % (stride * 4) == 0 else 2
            parts = [value] + [
                lax.ppermute(value, axis, [(i, i ^ j * stride) for i in range(count)])
                for j in range(1, group)
            ]
            stacked = jnp.stack(parts)
            member = position // stride % group
            ordered = [stacked[m ^ member] for m in range(group)]
            while len(ordered) > 1:
                ordered = [ordered[k] + ordered[k + 1] for k in range(0, len(ordered), 2)]
            value = ordered[0]
            stride *= group
    return value


def recurrence(rate, inflow, reverse):
    def advance(level, step):
        level = step[0] * level + step[1]
        return level, level

    start = jnp.zeros(inflow.shape[1:], inflow.dtype)
    return lax.scan(advance, start, (rate, inflow), reverse=reverse, unroll=8)[1]


def split_dot(value, mapping, along):
    parts = []
    rest = value
    for piece in range(3):
        part = lax.reduce_precision(rest, exponent_bits=8, mantissa_bits=7)
        parts.append(part.astype(jnp.bfloat16))
        rest = rest - part
    stacked = jnp.concatenate(parts, axis=0)
    out = lax.dot_general(
        stacked, mapping, (((1,), (along,)), ((), ())),
        preferred_element_type=jnp.float32,
    )
    rows = value.shape[0]
    return (out[:rows] + out[rows : 2 * rows]) + out[2 * rows :]


def masked_transpose_kernel(pattern_ref, factors_ref, out_ref):
    rows = factors_ref.shape[0] // BLK
    first = pl.program_id(0) * rows
    for row in range(rows):
        for col in range(factors_ref.shape[1] // BLK):
            keep = pattern_ref[first + row, col].astype(jnp.float32)
            tile = factors_ref[pl.ds(row * BLK, BLK), pl.ds(col * BLK, BLK)].astype(jnp.float32)
            out_ref[pl.ds(col * BLK, BLK), pl.ds(row * BLK, BLK)] = (tile.T * keep).astype(
                out_ref.dtype
            )


def masked_transpose(pattern, factors):
    lines, buses = factors.shape
    rows = 2 * BLK
    return pl.pallas_call(
        masked_transpose_kernel,
        out_shape=jax.ShapeDtypeStruct((buses, lines), factors.dtype),
        grid_spec=pltpu.PrefetchScalarGridSpec(
            num_scalar_prefetch=1,
            grid=(lines // rows,),
            in_specs=[pl.BlockSpec((rows, buses), lambda i, p: (i, 0))],
            out_specs=pl.BlockSpec((buses, rows), lambda i, p: (0, i)),
        ),
        interpret=INTERPRET,
    )(pattern, factors)


def on_device(
    load,
    ptdf,
    ptdf_pattern,
    line_limit,
    unit_bus,
    store_bus,
    tie_block,
    cost_quad,
    cost_lin,
    gen_limit,
    ramp_limit,
    retention,
    store_cap,
    gen_start,
    charge_start,
):
    highest = lax.Precision.HIGHEST
    demand = load[0]
    periods_here, scenarios, buses = demand.shape
    rows = periods_here * scenarios
    lines = ptdf.shape[1]
    stores = charge_start.shape[3]
    network_t = masked_transpose(ptdf_pattern[0], ptdf[0])
    bus_range = jnp.arange(buses, dtype=jnp.int32)
    device_bus = jnp.concatenate([unit_bus[0], store_bus[0]])
    device_map = (device_bus[:, None] == bus_range[None, :]).astype(jnp.bfloat16)
    units = unit_bus.shape[1]
    flow_cap = line_limit[0][None, :]
    ramp_cap = ramp_limit[0]
    quadratic = cost_quad[0]
    linear_cost = cost_lin[0]
    upper = gen_limit[0]
    capacity = store_cap[0]
    keep_rate = retention[0]
    demand_rows = demand.reshape(rows, buses)
    position = lax.axis_index("period")
    nbits = lax.axis_size("region").bit_length() - 1
    at_start = position == 0
    at_end = position == lax.axis_size("period") - 1
    first_here = position * periods_here
    rate_all = gathered(keep_rate, "period")
    rate_next = jnp.concatenate([rate_all[1:], jnp.zeros_like(rate_all[:1])])[:, None, :]
    rate_all = rate_all[:, None, :]
    charge_all = gathered(charge_start[0], "period")
    gen = gen_start[0]
    charge = charge_start[0]
    line_dual = jnp.zeros((rows, lines), jnp.float32)
    tie_dual = [jnp.zeros((rows, BLK), jnp.float32) for colour in range(COLORS)]
    ramp_dual = jnp.zeros_like(gen)
    ramp_dual_after = jnp.zeros_like(gen[0])
    store_dual = jnp.zeros_like(charge_all)
    balance_dual = jnp.zeros((rows,), jnp.float32)
    rho = jnp.float32(rho_start)
    for iteration in range(ITERS):
        gen_rows = gen.reshape(rows, -1)
        charge_rows = charge.reshape(rows, stores)
        inject = (
            split_dot(jnp.concatenate([gen_rows, -charge_rows], axis=1), device_map, 0)
            - demand_rows
        )
        flows = jnp.dot(
            inject.astype(jnp.bfloat16), network_t, preferred_element_type=jnp.float32
        )
        over = flows - jnp.clip(flows, -flow_cap, flow_cap)
        line_term = line_dual + rho * over
        flow_term = line_term
        local_primal = jnp.sum(over * over)
        new_ties = []
        for colour in range(COLORS):
            start = tie_block[0, colour] * BLK
            mine = lax.dynamic_slice_in_dim(flows, start, BLK, 1)
            theirs = swapped(mine, "region", colour % nbits)
            mismatch = mine + theirs
            tie_term = tie_dual[colour] + rho * mismatch
            current = lax.dynamic_slice_in_dim(flow_term, start, BLK, 1)
            flow_term = lax.dynamic_update_slice_in_dim(flow_term, current + tie_term, start, 1)
            local_primal = local_primal + jnp.sum(mismatch * mismatch)
            new_ties.append(tie_term)
        grad_inject = lax.dot_general(
            flow_term.astype(jnp.bfloat16),
            network_t,
            (((1,), (1,)), ((), ())),
            preferred_element_type=jnp.float32,
        )
        balance = jnp.mean(inject, axis=1)
        balance_term = balance_dual + rho * balance
        before = passed_along(gen[-1], "period", 1)
        following = passed_along(gen[0], "period", -1)
        earlier = jnp.concatenate([before[None], gen[:-1]], axis=0)
        change = gen - earlier
        ramp_over = change - jnp.clip(change, -ramp_cap, ramp_cap)
        ramp_over = jnp.concatenate(
            [jnp.where(at_start, 0.0, ramp_over[:1]), ramp_over[1:]], axis=0
        )
        ramp_term = ramp_dual + rho * ramp_over
        step_after = following - gen[-1]
        after = ramp_dual_after + rho * (step_after - jnp.clip(step_after, -ramp_cap, ramp_cap))
        after = jnp.where(at_end, 0.0, after)
        ramp_later = jnp.concatenate([ramp_term[1:], after[None]], axis=0)
        soc = recurrence(rate_all, charge_all, False)
        store_over_all = soc - jnp.clip(soc, 0.0, capacity)
        store_term_all = store_dual + rho * store_over_all
        adjoint_all = recurrence(rate_next, store_term_all, True)
        store_over = lax.dynamic_slice_in_dim(store_over_all, first_here, periods_here, 0)
        adjoint = lax.dynamic_slice_in_dim(adjoint_all, first_here, periods_here, 0)
        local_primal = (
            local_primal
            + jnp.sum(ramp_over * ramp_over)
            + jnp.sum(store_over * store_over)
            + jnp.sum(balance * balance)
        )
        push = split_dot(grad_inject, device_map, 1)
        unit_push = push[:, :units].reshape(gen.shape)
        store_push = push[:, units:].reshape(charge.shape)
        balance_wide = balance_term.reshape(periods_here, scenarios, 1)
        grad_gen = quadratic * gen + linear_cost + unit_push + balance_wide + ramp_term - ramp_later
        grad_charge = store_weight * charge + adjoint - store_push - balance_wide
        gen_next = jnp.clip(gen - step_size * grad_gen, 0.0, upper)
        charge_next = jnp.clip(charge - step_size * grad_charge, -0.25 * capacity, 0.25 * capacity)
        gen_step = gen_next - gen
        charge_step = charge_next - charge
        local_change = (jnp.sum(gen_step * gen_step) + jnp.sum(charge_step * charge_step)) / (
            step_size * step_size
        )
        partial = jnp.stack([local_primal, local_change])
        if iteration + 1 < ITERS:
            slab = jnp.pad(partial, (0, stores - 2))
            slab = jnp.broadcast_to(slab, (1, scenarios, stores))
            both = gathered(jnp.concatenate([charge_next, slab]), "period")
            both = both.reshape(-1, periods_here + 1, scenarios, stores)
            charge_all = both[:, :periods_here].reshape(-1, scenarios, stores)
            partial = jnp.sum(both[:, periods_here, 0, :2], axis=0)
            primal, changes = total(partial, ("region",))
        else:
            primal, changes = total(partial, ("region", "period"))
        line_dual = line_term
        tie_dual = new_ties
        ramp_dual = ramp_term
        ramp_dual_after = after
        store_dual = store_term_all
        balance_dual = balance_term
        rho = rho * ((primal + small_eps) / (changes + small_eps)) ** 0.25
        gen = gen_next
        charge = charge_next
    tie_out = jnp.concatenate(tie_dual, axis=1).reshape(periods_here, scenarios, COLORS * BLK)
    return (
        gen[None],
        charge[None],
        line_dual.reshape(periods_here, scenarios, lines)[None],
        tie_out[None],
        rho,
    )


def solution(mesh):
    return jax.shard_map(
        on_device,
        mesh=mesh,
        in_specs=(
            P("region", "period", None, None),
            P("region", None, None),
            P("region", None, None),
            P("region", None),
            P("region", None),
            P("region", None),
            P("region", None),
            P("region", None),
            P("region", None),
            P("region", None),
            P("region", None),
            P("region", "period", None),
            P("region", None),
            P("region", "period", None, None),
            P("region", "period", None, None),
        ),
        out_specs=(
            P("region", "period", None, None),
            P("region", "period", None, None),
            P("region", "period", None, None),
            P("region", "period", None, None),
            P(),
        ),
        check_vma=False,
    )
```

```python
import jax
import jax.numpy as jnp
from jax import lax
from jax.experimental import pallas as pl
from jax.experimental.pallas import tpu as pltpu
from jax.sharding import PartitionSpec as P

BLK = 128
COLORS = 4
ITERS = 2
INTERPRET = False


step_size = 0.05
store_weight = 0.1
rho_start = 1.0
small_eps = 1e-05


def swapped(shard, axis, apart):
    return lax.ppermute(shard, axis, [(i, i ^ 1 << apart) for i in range(lax.axis_size(axis))])


def passed_along(value, axis, steps):
    count = lax.axis_size(axis)
    leading, last = (max(0, -steps), min(count, count - steps))
    return lax.ppermute(value, axis, [(source, source + steps) for source in range(leading, last)])


def gathered(shard, axis):
    count, position = (lax.axis_size(axis), lax.axis_index(axis))
    whole, apart = (shard, 1)
    while apart < count:
        other = lax.ppermute(whole, axis, [(i, i ^ apart) for i in range(count)])
        low = position // apart % 2 == 0
        whole = jnp.where(low, jnp.concatenate([whole, other]), jnp.concatenate([other, whole]))
        apart *= 2
    return whole


def total(value, axes):
    for axis in axes:
        count, position = (lax.axis_size(axis), lax.axis_index(axis))
        stride = 1
        while stride < count:
            group = 4 if count % (stride * 4) == 0 else 2
            parts = [value] + [
                lax.ppermute(value, axis, [(i, i ^ j * stride) for i in range(count)])
                for j in range(1, group)
            ]
            stacked = jnp.stack(parts)
            member = position // stride % group
            ordered = [stacked[m ^ member] for m in range(group)]
            while len(ordered) > 1:
                ordered = [ordered[k] + ordered[k + 1] for k in range(0, len(ordered), 2)]
            value = ordered[0]
            stride *= group
    return value


def recurrence(rate, inflow, reverse):
    def advance(level, step):
        level = step[0] * level + step[1]
        return level, level

    start = jnp.zeros(inflow.shape[1:], inflow.dtype)
    return lax.scan(advance, start, (rate, inflow), reverse=reverse, unroll=8)[1]


def split_dot(value, mapping, along):
    parts = []
    rest = value
    for piece in range(3):
        part = lax.reduce_precision(rest, exponent_bits=8, mantissa_bits=7)
        parts.append(part.astype(jnp.bfloat16))
        rest = rest - part
    stacked = jnp.concatenate(parts, axis=0)
    out = lax.dot_general(
        stacked, mapping, (((1,), (along,)), ((), ())),
        preferred_element_type=jnp.float32,
    )
    rows = value.shape[0]
    return (out[:rows] + out[rows : 2 * rows]) + out[2 * rows :]


def masked_transpose_kernel(pattern_ref, factors_ref, out_ref):
    rows = factors_ref.shape[0] // BLK
    first = pl.program_id(0) * rows
    for row in range(rows):
        for col in range(factors_ref.shape[1] // BLK):
            keep = pattern_ref[first + row, col].astype(jnp.float32)
            tile = factors_ref[pl.ds(row * BLK, BLK), pl.ds(col * BLK, BLK)].astype(jnp.float32)
            out_ref[pl.ds(col * BLK, BLK), pl.ds(row * BLK, BLK)] = (tile.T * keep).astype(
                out_ref.dtype
            )


def masked_transpose(pattern, factors):
    lines, buses = factors.shape
    rows = 2 * BLK
    return pl.pallas_call(
        masked_transpose_kernel,
        out_shape=jax.ShapeDtypeStruct((buses, lines), factors.dtype),
        grid_spec=pltpu.PrefetchScalarGridSpec(
            num_scalar_prefetch=1,
            grid=(lines // rows,),
            in_specs=[pl.BlockSpec((rows, buses), lambda i, p: (i, 0))],
            out_specs=pl.BlockSpec((buses, rows), lambda i, p: (0, i)),
        ),
        interpret=INTERPRET,
    )(pattern, factors)


def on_device(
    load,
    ptdf,
    ptdf_pattern,
    line_limit,
    unit_bus,
    store_bus,
    tie_block,
    cost_quad,
    cost_lin,
    gen_limit,
    ramp_limit,
    retention,
    store_cap,
    gen_start,
    charge_start,
):
    highest = lax.Precision.HIGHEST
    demand = load[0]
    periods_here, scenarios, buses = demand.shape
    rows = periods_here * scenarios
    lines = ptdf.shape[1]
    stores = charge_start.shape[3]
    network_t = masked_transpose(ptdf_pattern[0], ptdf[0])
    bus_range = jnp.arange(buses, dtype=jnp.int32)
    device_bus = jnp.concatenate([unit_bus[0], store_bus[0]])
    device_map = (device_bus[:, None] == bus_range[None, :]).astype(jnp.bfloat16)
    units = unit_bus.shape[1]
    flow_cap = line_limit[0][None, :]
    ramp_cap = ramp_limit[0]
    quadratic = cost_quad[0]
    linear_cost = cost_lin[0]
    upper = gen_limit[0]
    capacity = store_cap[0]
    keep_rate = retention[0]
    demand_rows = demand.reshape(rows, buses)
    position = lax.axis_index("period")
    nbits = lax.axis_size("region").bit_length() - 1
    at_start = position == 0
    at_end = position == lax.axis_size("period") - 1
    first_here = position * periods_here
    rate_slab = jnp.pad(keep_rate, ((0, scenarios - periods_here), (0, 0)))[None]
    both = gathered(jnp.concatenate([charge_start[0], rate_slab]), "period")
    both = both.reshape(-1, periods_here + 1, scenarios, stores)
    charge_all = both[:, :periods_here].reshape(-1, scenarios, stores)
    rate_all = both[:, periods_here, :periods_here].reshape(-1, stores)
    rate_next = jnp.concatenate([rate_all[1:], jnp.zeros_like(rate_all[:1])])[:, None, :]
    rate_all = rate_all[:, None, :]
    gen = gen_start[0]
    charge = charge_start[0]
    line_dual = jnp.zeros((rows, lines), jnp.float32)
    tie_dual = [jnp.zeros((rows, BLK), jnp.float32) for colour in range(COLORS)]
    ramp_dual = jnp.zeros_like(gen)
    ramp_dual_after = jnp.zeros_like(gen[0])
    store_dual = jnp.zeros_like(charge_all)
    balance_dual = jnp.zeros((rows,), jnp.float32)
    rho = jnp.float32(rho_start)
    for iteration in range(ITERS):
        gen_rows = gen.reshape(rows, -1)
        charge_rows = charge.reshape(rows, stores)
        inject = (
            split_dot(jnp.concatenate([gen_rows, -charge_rows], axis=1), device_map, 0)
            - demand_rows
        )
        flows = jnp.dot(
            inject.astype(jnp.bfloat16), network_t, preferred_element_type=jnp.float32
        )
        over = flows - jnp.clip(flows, -flow_cap, flow_cap)
        line_term = line_dual + rho * over
        flow_term = line_term
        local_primal = jnp.sum(over * over)
        new_ties = []
        for colour in range(COLORS):
            start = tie_block[0, colour] * BLK
            mine = lax.dynamic_slice_in_dim(flows, start, BLK, 1)
            theirs = swapped(mine, "region", colour % nbits)
            mismatch = mine + theirs
            tie_term = tie_dual[colour] + rho * mismatch
            current = lax.dynamic_slice_in_dim(flow_term, start, BLK, 1)
            flow_term = lax.dynamic_update_slice_in_dim(flow_term, current + tie_term, start, 1)
            local_primal = local_primal + jnp.sum(mismatch * mismatch)
            new_ties.append(tie_term)
        grad_inject = lax.dot_general(
            flow_term.astype(jnp.bfloat16),
            network_t,
            (((1,), (1,)), ((), ())),
            preferred_element_type=jnp.float32,
        )
        balance = jnp.mean(inject, axis=1)
        balance_term = balance_dual + rho * balance
        before = passed_along(gen[-1], "period", 1)
        following = passed_along(gen[0], "period", -1)
        earlier = jnp.concatenate([before[None], gen[:-1]], axis=0)
        change = gen - earlier
        ramp_over = change - jnp.clip(change, -ramp_cap, ramp_cap)
        ramp_over = jnp.concatenate(
            [jnp.where(at_start, 0.0, ramp_over[:1]), ramp_over[1:]], axis=0
        )
        ramp_term = ramp_dual + rho * ramp_over
        step_after = following - gen[-1]
        after = ramp_dual_after + rho * (step_after - jnp.clip(step_after, -ramp_cap, ramp_cap))
        after = jnp.where(at_end, 0.0, after)
        ramp_later = jnp.concatenate([ramp_term[1:], after[None]], axis=0)
        soc = recurrence(rate_all, charge_all, False)
        store_over_all = soc - jnp.clip(soc, 0.0, capacity)
        store_term_all = store_dual + rho * store_over_all
        adjoint_all = recurrence(rate_next, store_term_all, True)
        store_over = lax.dynamic_slice_in_dim(store_over_all, first_here, periods_here, 0)
        adjoint = lax.dynamic_slice_in_dim(adjoint_all, first_here, periods_here, 0)
        local_primal = (
            local_primal
            + jnp.sum(ramp_over * ramp_over)
            + jnp.sum(store_over * store_over)
            + jnp.sum(balance * balance)
        )
        push = split_dot(grad_inject, device_map, 1)
        unit_push = push[:, :units].reshape(gen.shape)
        store_push = push[:, units:].reshape(charge.shape)
        balance_wide = balance_term.reshape(periods_here, scenarios, 1)
        grad_gen = quadratic * gen + linear_cost + unit_push + balance_wide + ramp_term - ramp_later
        grad_charge = store_weight * charge + adjoint - store_push - balance_wide
        gen_next = jnp.clip(gen - step_size * grad_gen, 0.0, upper)
        charge_next = jnp.clip(charge - step_size * grad_charge, -0.25 * capacity, 0.25 * capacity)
        gen_step = gen_next - gen
        charge_step = charge_next - charge
        local_change = (jnp.sum(gen_step * gen_step) + jnp.sum(charge_step * charge_step)) / (
            step_size * step_size
        )
        partial = jnp.stack([local_primal, local_change])
        if iteration + 1 < ITERS:
            slab = jnp.pad(partial, (0, stores - 2))
            slab = jnp.broadcast_to(slab, (1, scenarios, stores))
            both = gathered(jnp.concatenate([charge_next, slab]), "period")
            both = both.reshape(-1, periods_here + 1, scenarios, stores)
            charge_all = both[:, :periods_here].reshape(-1, scenarios, stores)
            partial = jnp.sum(both[:, periods_here, 0, :2], axis=0)
            primal, changes = total(partial, ("region",))
        else:
            primal, changes = total(partial, ("region", "period"))
        line_dual = line_term
        tie_dual = new_ties
        ramp_dual = ramp_term
        ramp_dual_after = after
        store_dual = store_term_all
        balance_dual = balance_term
        rho = rho * ((primal + small_eps) / (changes + small_eps)) ** 0.25
        gen = gen_next
        charge = charge_next
    tie_out = jnp.concatenate(tie_dual, axis=1).reshape(periods_here, scenarios, COLORS * BLK)
    return (
        gen[None],
        charge[None],
        line_dual.reshape(periods_here, scenarios, lines)[None],
        tie_out[None],
        rho,
    )


def solution(mesh):
    return jax.shard_map(
        on_device,
        mesh=mesh,
        in_specs=(
            P("region", "period", None, None),
            P("region", None, None),
            P("region", None, None),
            P("region", None),
            P("region", None),
            P("region", None),
            P("region", None),
            P("region", None),
            P("region", None),
            P("region", None),
            P("region", None),
            P("region", "period", None),
            P("region", None),
            P("region", "period", None, None),
            P("region", "period", None, None),
        ),
        out_specs=(
            P("region", "period", None, None),
            P("region", "period", None, None),
            P("region", "period", None, None),
            P("region", "period", None, None),
            P(),
        ),
        check_vma=False,
    )
```

```python
import jax
import jax.numpy as jnp
from jax import lax
from jax.experimental import pallas as pl
from jax.experimental.pallas import tpu as pltpu
from jax.sharding import PartitionSpec as P

BLK = 128
COLORS = 4
ITERS = 2
INTERPRET = False


step_size = 0.05
store_weight = 0.1
rho_start = 1.0
small_eps = 1e-05


def swapped(shard, axis, apart):
    return lax.ppermute(shard, axis, [(i, i ^ 1 << apart) for i in range(lax.axis_size(axis))])


def passed_along(value, axis, steps):
    count = lax.axis_size(axis)
    leading, last = (max(0, -steps), min(count, count - steps))
    return lax.ppermute(value, axis, [(source, source + steps) for source in range(leading, last)])


def gathered(shard, axis):
    count, position = (lax.axis_size(axis), lax.axis_index(axis))
    whole, stride = (shard, 1)
    while stride < count:
        group = 4 if count % (stride * 4) == 0 else 2
        parts = [whole] + [
            lax.ppermute(whole, axis, [(i, i ^ j * stride) for i in range(count)])
            for j in range(1, group)
        ]
        stacked = jnp.stack(parts)
        member = position // stride % group
        whole = jnp.concatenate([stacked[m ^ member] for m in range(group)])
        stride *= group
    return whole


def total(value, axes):
    for axis in axes:
        count, position = (lax.axis_size(axis), lax.axis_index(axis))
        stride = 1
        while stride < count:
            group = 4 if count % (stride * 4) == 0 else 2
            parts = [value] + [
                lax.ppermute(value, axis, [(i, i ^ j * stride) for i in range(count)])
                for j in range(1, group)
            ]
            stacked = jnp.stack(parts)
            member = position // stride % group
            ordered = [stacked[m ^ member] for m in range(group)]
            while len(ordered) > 1:
                ordered = [ordered[k] + ordered[k + 1] for k in range(0, len(ordered), 2)]
            value = ordered[0]
            stride *= group
    return value


def recurrence(rate, inflow, reverse):
    def advance(level, step):
        level = step[0] * level + step[1]
        return level, level

    start = jnp.zeros(inflow.shape[1:], inflow.dtype)
    return lax.scan(advance, start, (rate, inflow), reverse=reverse, unroll=8)[1]


def split_dot(value, mapping, along):
    parts = []
    rest = value
    for piece in range(3):
        part = lax.reduce_precision(rest, exponent_bits=8, mantissa_bits=7)
        parts.append(part.astype(jnp.bfloat16))
        rest = rest - part
    stacked = jnp.concatenate(parts, axis=0)
    out = lax.dot_general(
        stacked, mapping, (((1,), (along,)), ((), ())),
        preferred_element_type=jnp.float32,
    )
    rows = value.shape[0]
    return (out[:rows] + out[rows : 2 * rows]) + out[2 * rows :]


def masked_transpose_kernel(pattern_ref, factors_ref, out_ref):
    rows = factors_ref.shape[0] // BLK
    first = pl.program_id(0) * rows
    for row in range(rows):
        for col in range(factors_ref.shape[1] // BLK):
            keep = pattern_ref[first + row, col].astype(jnp.float32)
            tile = factors_ref[pl.ds(row * BLK, BLK), pl.ds(col * BLK, BLK)].astype(jnp.float32)
            out_ref[pl.ds(col * BLK, BLK), pl.ds(row * BLK, BLK)] = (tile.T * keep).astype(
                out_ref.dtype
            )


def masked_transpose(pattern, factors):
    lines, buses = factors.shape
    rows = 2 * BLK
    return pl.pallas_call(
        masked_transpose_kernel,
        out_shape=jax.ShapeDtypeStruct((buses, lines), factors.dtype),
        grid_spec=pltpu.PrefetchScalarGridSpec(
            num_scalar_prefetch=1,
            grid=(lines // rows,),
            in_specs=[pl.BlockSpec((rows, buses), lambda i, p: (i, 0))],
            out_specs=pl.BlockSpec((buses, rows), lambda i, p: (0, i)),
        ),
        interpret=INTERPRET,
    )(pattern, factors)


def on_device(
    load,
    ptdf,
    ptdf_pattern,
    line_limit,
    unit_bus,
    store_bus,
    tie_block,
    cost_quad,
    cost_lin,
    gen_limit,
    ramp_limit,
    retention,
    store_cap,
    gen_start,
    charge_start,
):
    highest = lax.Precision.HIGHEST
    demand = load[0]
    periods_here, scenarios, buses = demand.shape
    rows = periods_here * scenarios
    lines = ptdf.shape[1]
    stores = charge_start.shape[3]
    network_t = masked_transpose(ptdf_pattern[0], ptdf[0])
    bus_range = jnp.arange(buses, dtype=jnp.int32)
    device_bus = jnp.concatenate([unit_bus[0], store_bus[0]])
    device_map = (device_bus[:, None] == bus_range[None, :]).astype(jnp.bfloat16)
    units = unit_bus.shape[1]
    flow_cap = line_limit[0][None, :]
    ramp_cap = ramp_limit[0]
    quadratic = cost_quad[0]
    linear_cost = cost_lin[0]
    upper = gen_limit[0]
    capacity = store_cap[0]
    keep_rate = retention[0]
    demand_rows = demand.reshape(rows, buses)
    position = lax.axis_index("period")
    nbits = lax.axis_size("region").bit_length() - 1
    at_start = position == 0
    at_end = position == lax.axis_size("period") - 1
    first_here = position * periods_here
    rate_slab = jnp.pad(keep_rate, ((0, scenarios - periods_here), (0, 0)))[None]
    both = gathered(jnp.concatenate([charge_start[0], rate_slab]), "period")
    both = both.reshape(-1, periods_here + 1, scenarios, stores)
    charge_all = both[:, :periods_here].reshape(-1, scenarios, stores)
    rate_all = both[:, periods_here, :periods_here].reshape(-1, stores)
    rate_next = jnp.concatenate([rate_all[1:], jnp.zeros_like(rate_all[:1])])[:, None, :]
    rate_all = rate_all[:, None, :]
    gen = gen_start[0]
    charge = charge_start[0]
    line_dual = jnp.zeros((rows, lines), jnp.float32)
    tie_dual = [jnp.zeros((rows, BLK), jnp.float32) for colour in range(COLORS)]
    ramp_dual = jnp.zeros_like(gen)
    ramp_dual_after = jnp.zeros_like(gen[0])
    store_dual = jnp.zeros_like(charge_all)
    balance_dual = jnp.zeros((rows,), jnp.float32)
    rho = jnp.float32(rho_start)
    for iteration in range(ITERS):
        gen_rows = gen.reshape(rows, -1)
        charge_rows = charge.reshape(rows, stores)
        inject = (
            split_dot(jnp.concatenate([gen_rows, -charge_rows], axis=1), device_map, 0)
            - demand_rows
        )
        flows = jnp.dot(
            inject.astype(jnp.bfloat16), network_t, preferred_element_type=jnp.float32
        )
        over = flows - jnp.clip(flows, -flow_cap, flow_cap)
        line_term = line_dual + rho * over
        flow_term = line_term
        local_primal = jnp.sum(over * over)
        new_ties = []
        for colour in range(COLORS):
            start = tie_block[0, colour] * BLK
            mine = lax.dynamic_slice_in_dim(flows, start, BLK, 1)
            theirs = swapped(mine, "region", colour % nbits)
            mismatch = mine + theirs
            tie_term = tie_dual[colour] + rho * mismatch
            current = lax.dynamic_slice_in_dim(flow_term, start, BLK, 1)
            flow_term = lax.dynamic_update_slice_in_dim(flow_term, current + tie_term, start, 1)
            local_primal = local_primal + jnp.sum(mismatch * mismatch)
            new_ties.append(tie_term)
        grad_inject = lax.dot_general(
            flow_term.astype(jnp.bfloat16),
            network_t,
            (((1,), (1,)), ((), ())),
            preferred_element_type=jnp.float32,
        )
        balance = jnp.mean(inject, axis=1)
        balance_term = balance_dual + rho * balance
        before = passed_along(gen[-1], "period", 1)
        following = passed_along(gen[0], "period", -1)
        earlier = jnp.concatenate([before[None], gen[:-1]], axis=0)
        change = gen - earlier
        ramp_over = change - jnp.clip(change, -ramp_cap, ramp_cap)
        ramp_over = jnp.concatenate(
            [jnp.where(at_start, 0.0, ramp_over[:1]), ramp_over[1:]], axis=0
        )
        ramp_term = ramp_dual + rho * ramp_over
        step_after = following - gen[-1]
        after = ramp_dual_after + rho * (step_after - jnp.clip(step_after, -ramp_cap, ramp_cap))
        after = jnp.where(at_end, 0.0, after)
        ramp_later = jnp.concatenate([ramp_term[1:], after[None]], axis=0)
        soc = recurrence(rate_all, charge_all, False)
        store_over_all = soc - jnp.clip(soc, 0.0, capacity)
        store_term_all = store_dual + rho * store_over_all
        adjoint_all = recurrence(rate_next, store_term_all, True)
        store_over = lax.dynamic_slice_in_dim(store_over_all, first_here, periods_here, 0)
        adjoint = lax.dynamic_slice_in_dim(adjoint_all, first_here, periods_here, 0)
        local_primal = (
            local_primal
            + jnp.sum(ramp_over * ramp_over)
            + jnp.sum(store_over * store_over)
            + jnp.sum(balance * balance)
        )
        push = split_dot(grad_inject, device_map, 1)
        unit_push = push[:, :units].reshape(gen.shape)
        store_push = push[:, units:].reshape(charge.shape)
        balance_wide = balance_term.reshape(periods_here, scenarios, 1)
        grad_gen = quadratic * gen + linear_cost + unit_push + balance_wide + ramp_term - ramp_later
        grad_charge = store_weight * charge + adjoint - store_push - balance_wide
        gen_next = jnp.clip(gen - step_size * grad_gen, 0.0, upper)
        charge_next = jnp.clip(charge - step_size * grad_charge, -0.25 * capacity, 0.25 * capacity)
        gen_step = gen_next - gen
        charge_step = charge_next - charge
        local_change = (jnp.sum(gen_step * gen_step) + jnp.sum(charge_step * charge_step)) / (
            step_size * step_size
        )
        partial = jnp.stack([local_primal, local_change])
        if iteration + 1 < ITERS:
            slab = jnp.pad(partial, (0, stores - 2))
            slab = jnp.broadcast_to(slab, (1, scenarios, stores))
            both = gathered(jnp.concatenate([charge_next, slab]), "period")
            both = both.reshape(-1, periods_here + 1, scenarios, stores)
            charge_all = both[:, :periods_here].reshape(-1, scenarios, stores)
            partial = jnp.sum(both[:, periods_here, 0, :2], axis=0)
            primal, changes = total(partial, ("region",))
        else:
            primal, changes = total(partial, ("region", "period"))
        line_dual = line_term
        tie_dual = new_ties
        ramp_dual = ramp_term
        ramp_dual_after = after
        store_dual = store_term_all
        balance_dual = balance_term
        rho = rho * ((primal + small_eps) / (changes + small_eps)) ** 0.25
        gen = gen_next
        charge = charge_next
    tie_out = jnp.concatenate(tie_dual, axis=1).reshape(periods_here, scenarios, COLORS * BLK)
    return (
        gen[None],
        charge[None],
        line_dual.reshape(periods_here, scenarios, lines)[None],
        tie_out[None],
        rho,
    )


def solution(mesh):
    return jax.shard_map(
        on_device,
        mesh=mesh,
        in_specs=(
            P("region", "period", None, None),
            P("region", None, None),
            P("region", None, None),
            P("region", None),
            P("region", None),
            P("region", None),
            P("region", None),
            P("region", None),
            P("region", None),
            P("region", None),
            P("region", None),
            P("region", "period", None),
            P("region", None),
            P("region", "period", None, None),
            P("region", "period", None, None),
        ),
        out_specs=(
            P("region", "period", None, None),
            P("region", "period", None, None),
            P("region", "period", None, None),
            P("region", "period", None, None),
            P(),
        ),
        check_vma=False,
    )
```

```python
import jax
import jax.numpy as jnp
from jax import lax
from jax.experimental import pallas as pl
from jax.experimental.pallas import tpu as pltpu
from jax.sharding import PartitionSpec as P

BLK = 128
COLORS = 4
ITERS = 2
INTERPRET = False


step_size = 0.05
store_weight = 0.1
rho_start = 1.0
small_eps = 1e-05


def swapped(shard, axis, apart):
    return lax.ppermute(shard, axis, [(i, i ^ 1 << apart) for i in range(lax.axis_size(axis))])


def passed_along(value, axis, steps):
    count = lax.axis_size(axis)
    leading, last = (max(0, -steps), min(count, count - steps))
    return lax.ppermute(value, axis, [(source, source + steps) for source in range(leading, last)])


def gathered(shard, axis):
    count, position = (lax.axis_size(axis), lax.axis_index(axis))
    whole, stride = (shard, 1)
    while stride < count:
        group = 4 if count % (stride * 4) == 0 else 2
        parts = [whole] + [
            lax.ppermute(whole, axis, [(i, i ^ j * stride) for i in range(count)])
            for j in range(1, group)
        ]
        stacked = jnp.stack(parts)
        member = position // stride % group
        whole = jnp.concatenate([stacked[m ^ member] for m in range(group)])
        stride *= group
    return whole


def total(value, axes):
    for axis in axes:
        count, position = (lax.axis_size(axis), lax.axis_index(axis))
        stride = 1
        while stride < count:
            group = 4 if count % (stride * 4) == 0 else 2
            parts = [value] + [
                lax.ppermute(value, axis, [(i, i ^ j * stride) for i in range(count)])
                for j in range(1, group)
            ]
            stacked = jnp.stack(parts)
            member = position // stride % group
            ordered = [stacked[m ^ member] for m in range(group)]
            while len(ordered) > 1:
                ordered = [ordered[k] + ordered[k + 1] for k in range(0, len(ordered), 2)]
            value = ordered[0]
            stride *= group
    return value


def recurrence(rate, inflow, reverse):
    def advance(level, step):
        level = step[0] * level + step[1]
        return level, level

    start = jnp.zeros(inflow.shape[1:], inflow.dtype)
    return lax.scan(advance, start, (rate, inflow), reverse=reverse, unroll=8)[1]


def split_dot(value, mapping, along):
    parts = []
    rest = value
    for piece in range(3):
        part = lax.reduce_precision(rest, exponent_bits=8, mantissa_bits=7)
        parts.append(part.astype(jnp.bfloat16))
        rest = rest - part
    stacked = jnp.concatenate(parts, axis=0)
    out = lax.dot_general(
        stacked, mapping, (((1,), (along,)), ((), ())),
        preferred_element_type=jnp.float32,
    )
    rows = value.shape[0]
    return (out[:rows] + out[rows : 2 * rows]) + out[2 * rows :]


def masked_transpose_kernel(pattern_ref, factors_ref, out_ref):
    rows = factors_ref.shape[0] // BLK
    first = pl.program_id(0) * rows
    for row in range(rows):
        for col in range(factors_ref.shape[1] // BLK):
            keep = pattern_ref[first + row, col].astype(jnp.float32).astype(factors_ref.dtype)
            tile = factors_ref[pl.ds(row * BLK, BLK), pl.ds(col * BLK, BLK)]
            out_ref[pl.ds(col * BLK, BLK), pl.ds(row * BLK, BLK)] = tile.T * keep


def masked_transpose(pattern, factors):
    lines, buses = factors.shape
    rows = 2 * BLK
    return pl.pallas_call(
        masked_transpose_kernel,
        out_shape=jax.ShapeDtypeStruct((buses, lines), factors.dtype),
        grid_spec=pltpu.PrefetchScalarGridSpec(
            num_scalar_prefetch=1,
            grid=(lines // rows,),
            in_specs=[pl.BlockSpec((rows, buses), lambda i, p: (i, 0))],
            out_specs=pl.BlockSpec((buses, rows), lambda i, p: (0, i)),
        ),
        interpret=INTERPRET,
    )(pattern, factors)


def on_device(
    load,
    ptdf,
    ptdf_pattern,
    line_limit,
    unit_bus,
    store_bus,
    tie_block,
    cost_quad,
    cost_lin,
    gen_limit,
    ramp_limit,
    retention,
    store_cap,
    gen_start,
    charge_start,
):
    highest = lax.Precision.HIGHEST
    demand = load[0]
    periods_here, scenarios, buses = demand.shape
    rows = periods_here * scenarios
    lines = ptdf.shape[1]
    stores = charge_start.shape[3]
    network_t = masked_transpose(ptdf_pattern[0], ptdf[0])
    bus_range = jnp.arange(buses, dtype=jnp.int32)
    device_bus = jnp.concatenate([unit_bus[0], store_bus[0]])
    device_map = (device_bus[:, None] == bus_range[None, :]).astype(jnp.bfloat16)
    units = unit_bus.shape[1]
    flow_cap = line_limit[0][None, :]
    ramp_cap = ramp_limit[0]
    quadratic = cost_quad[0]
    linear_cost = cost_lin[0]
    upper = gen_limit[0]
    capacity = store_cap[0]
    keep_rate = retention[0]
    demand_rows = demand.reshape(rows, buses)
    position = lax.axis_index("period")
    nbits = lax.axis_size("region").bit_length() - 1
    at_start = position == 0
    at_end = position == lax.axis_size("period") - 1
    first_here = position * periods_here
    rate_slab = jnp.pad(keep_rate, ((0, scenarios - periods_here), (0, 0)))[None]
    both = gathered(jnp.concatenate([charge_start[0], rate_slab]), "period")
    both = both.reshape(-1, periods_here + 1, scenarios, stores)
    charge_all = both[:, :periods_here].reshape(-1, scenarios, stores)
    rate_all = both[:, periods_here, :periods_here].reshape(-1, stores)
    rate_next = jnp.concatenate([rate_all[1:], jnp.zeros_like(rate_all[:1])])[:, None, :]
    rate_all = rate_all[:, None, :]
    gen = gen_start[0]
    charge = charge_start[0]
    line_dual = jnp.zeros((rows, lines), jnp.float32)
    tie_dual = [jnp.zeros((rows, BLK), jnp.float32) for colour in range(COLORS)]
    ramp_dual = jnp.zeros_like(gen)
    ramp_dual_after = jnp.zeros_like(gen[0])
    store_dual = jnp.zeros_like(charge_all)
    balance_dual = jnp.zeros((rows,), jnp.float32)
    rho = jnp.float32(rho_start)
    for iteration in range(ITERS):
        gen_rows = gen.reshape(rows, -1)
        charge_rows = charge.reshape(rows, stores)
        inject = (
            split_dot(jnp.concatenate([gen_rows, -charge_rows], axis=1), device_map, 0)
            - demand_rows
        )
        flows = jnp.dot(
            inject.astype(jnp.bfloat16), network_t, preferred_element_type=jnp.float32
        )
        over = flows - jnp.clip(flows, -flow_cap, flow_cap)
        line_term = line_dual + rho * over
        flow_term = line_term
        local_primal = jnp.sum(over * over)
        new_ties = []
        for colour in range(COLORS):
            start = tie_block[0, colour] * BLK
            mine = lax.dynamic_slice_in_dim(flows, start, BLK, 1)
            theirs = swapped(mine, "region", colour % nbits)
            mismatch = mine + theirs
            tie_term = tie_dual[colour] + rho * mismatch
            current = lax.dynamic_slice_in_dim(flow_term, start, BLK, 1)
            flow_term = lax.dynamic_update_slice_in_dim(flow_term, current + tie_term, start, 1)
            local_primal = local_primal + jnp.sum(mismatch * mismatch)
            new_ties.append(tie_term)
        grad_inject = lax.dot_general(
            flow_term.astype(jnp.bfloat16),
            network_t,
            (((1,), (1,)), ((), ())),
            preferred_element_type=jnp.float32,
        )
        balance = jnp.mean(inject, axis=1)
        balance_term = balance_dual + rho * balance
        before = passed_along(gen[-1], "period", 1)
        following = passed_along(gen[0], "period", -1)
        earlier = jnp.concatenate([before[None], gen[:-1]], axis=0)
        change = gen - earlier
        ramp_over = change - jnp.clip(change, -ramp_cap, ramp_cap)
        ramp_over = jnp.concatenate(
            [jnp.where(at_start, 0.0, ramp_over[:1]), ramp_over[1:]], axis=0
        )
        ramp_term = ramp_dual + rho * ramp_over
        step_after = following - gen[-1]
        after = ramp_dual_after + rho * (step_after - jnp.clip(step_after, -ramp_cap, ramp_cap))
        after = jnp.where(at_end, 0.0, after)
        ramp_later = jnp.concatenate([ramp_term[1:], after[None]], axis=0)
        soc = recurrence(rate_all, charge_all, False)
        store_over_all = soc - jnp.clip(soc, 0.0, capacity)
        store_term_all = store_dual + rho * store_over_all
        adjoint_all = recurrence(rate_next, store_term_all, True)
        store_over = lax.dynamic_slice_in_dim(store_over_all, first_here, periods_here, 0)
        adjoint = lax.dynamic_slice_in_dim(adjoint_all, first_here, periods_here, 0)
        local_primal = (
            local_primal
            + jnp.sum(ramp_over * ramp_over)
            + jnp.sum(store_over * store_over)
            + jnp.sum(balance * balance)
        )
        push = split_dot(grad_inject, device_map, 1)
        unit_push = push[:, :units].reshape(gen.shape)
        store_push = push[:, units:].reshape(charge.shape)
        balance_wide = balance_term.reshape(periods_here, scenarios, 1)
        grad_gen = quadratic * gen + linear_cost + unit_push + balance_wide + ramp_term - ramp_later
        grad_charge = store_weight * charge + adjoint - store_push - balance_wide
        gen_next = jnp.clip(gen - step_size * grad_gen, 0.0, upper)
        charge_next = jnp.clip(charge - step_size * grad_charge, -0.25 * capacity, 0.25 * capacity)
        gen_step = gen_next - gen
        charge_step = charge_next - charge
        local_change = (jnp.sum(gen_step * gen_step) + jnp.sum(charge_step * charge_step)) / (
            step_size * step_size
        )
        partial = jnp.stack([local_primal, local_change])
        if iteration + 1 < ITERS:
            slab = jnp.pad(partial, (0, stores - 2))
            slab = jnp.broadcast_to(slab, (1, scenarios, stores))
            both = gathered(jnp.concatenate([charge_next, slab]), "period")
            both = both.reshape(-1, periods_here + 1, scenarios, stores)
            charge_all = both[:, :periods_here].reshape(-1, scenarios, stores)
            partial = jnp.sum(both[:, periods_here, 0, :2], axis=0)
            primal, changes = total(partial, ("region",))
        else:
            primal, changes = total(partial, ("region", "period"))
        line_dual = line_term
        tie_dual = new_ties
        ramp_dual = ramp_term
        ramp_dual_after = after
        store_dual = store_term_all
        balance_dual = balance_term
        rho = rho * ((primal + small_eps) / (changes + small_eps)) ** 0.25
        gen = gen_next
        charge = charge_next
    tie_out = jnp.concatenate(tie_dual, axis=1).reshape(periods_here, scenarios, COLORS * BLK)
    return (
        gen[None],
        charge[None],
        line_dual.reshape(periods_here, scenarios, lines)[None],
        tie_out[None],
        rho,
    )


def solution(mesh):
    return jax.shard_map(
        on_device,
        mesh=mesh,
        in_specs=(
            P("region", "period", None, None),
            P("region", None, None),
            P("region", None, None),
            P("region", None),
            P("region", None),
            P("region", None),
            P("region", None),
            P("region", None),
            P("region", None),
            P("region", None),
            P("region", None),
            P("region", "period", None),
            P("region", None),
            P("region", "period", None, None),
            P("region", "period", None, None),
        ),
        out_specs=(
            P("region", "period", None, None),
            P("region", "period", None, None),
            P("region", "period", None, None),
            P("region", "period", None, None),
            P(),
        ),
        check_vma=False,
    )
```

```python
import jax
import jax.numpy as jnp
from jax import lax
from jax.experimental import pallas as pl
from jax.experimental.pallas import tpu as pltpu
from jax.sharding import PartitionSpec as P

BLK = 128
COLORS = 4
ITERS = 2
INTERPRET = False


step_size = 0.05
store_weight = 0.1
rho_start = 1.0
small_eps = 1e-05


def swapped(shard, axis, apart):
    return lax.ppermute(shard, axis, [(i, i ^ 1 << apart) for i in range(lax.axis_size(axis))])


def passed_along(value, axis, steps):
    count = lax.axis_size(axis)
    leading, last = (max(0, -steps), min(count, count - steps))
    return lax.ppermute(value, axis, [(source, source + steps) for source in range(leading, last)])


def gathered(shard, axis):
    count, position = (lax.axis_size(axis), lax.axis_index(axis))
    whole, stride = (shard, 1)
    while stride < count:
        group = 4 if count % (stride * 4) == 0 else 2
        parts = [whole] + [
            lax.ppermute(whole, axis, [(i, i ^ j * stride) for i in range(count)])
            for j in range(1, group)
        ]
        stacked = jnp.stack(parts)
        member = position // stride % group
        whole = jnp.concatenate([stacked[m ^ member] for m in range(group)])
        stride *= group
    return whole


def total(value, axes):
    for axis in axes:
        count, position = (lax.axis_size(axis), lax.axis_index(axis))
        stride = 1
        while stride < count:
            group = 4 if count % (stride * 4) == 0 else 2
            parts = [value] + [
                lax.ppermute(value, axis, [(i, i ^ j * stride) for i in range(count)])
                for j in range(1, group)
            ]
            stacked = jnp.stack(parts)
            member = position // stride % group
            ordered = [stacked[m ^ member] for m in range(group)]
            while len(ordered) > 1:
                ordered = [ordered[k] + ordered[k + 1] for k in range(0, len(ordered), 2)]
            value = ordered[0]
            stride *= group
    return value


def recurrence(rate, inflow, reverse):
    def advance(level, step):
        level = step[0] * level + step[1]
        return level, level

    start = jnp.zeros(inflow.shape[1:], inflow.dtype)
    return lax.scan(advance, start, (rate, inflow), reverse=reverse, unroll=8)[1]


def split_dot(value, mapping, along):
    parts = []
    rest = value
    for piece in range(3):
        part = lax.reduce_precision(rest, exponent_bits=8, mantissa_bits=7)
        parts.append(part.astype(jnp.bfloat16))
        rest = rest - part
    stacked = jnp.concatenate(parts, axis=0)
    out = lax.dot_general(
        stacked, mapping, (((1,), (along,)), ((), ())),
        preferred_element_type=jnp.float32,
    )
    rows = value.shape[0]
    return (out[:rows] + out[rows : 2 * rows]) + out[2 * rows :]


def masked_transpose_kernel(pattern_ref, factors_ref, out_ref):
    rows = factors_ref.shape[0] // BLK
    first = pl.program_id(0) * rows
    for row in range(rows):
        for col in range(factors_ref.shape[1] // BLK):
            keep = pattern_ref[first + row, col].astype(jnp.float32).astype(factors_ref.dtype)
            tile = factors_ref[pl.ds(row * BLK, BLK), pl.ds(col * BLK, BLK)]
            out_ref[pl.ds(col * BLK, BLK), pl.ds(row * BLK, BLK)] = tile.T * keep


def masked_transpose(pattern, factors):
    lines, buses = factors.shape
    rows = 4 * BLK
    return pl.pallas_call(
        masked_transpose_kernel,
        out_shape=jax.ShapeDtypeStruct((buses, lines), factors.dtype),
        grid_spec=pltpu.PrefetchScalarGridSpec(
            num_scalar_prefetch=1,
            grid=(lines // rows,),
            in_specs=[pl.BlockSpec((rows, buses), lambda i, p: (i, 0))],
            out_specs=pl.BlockSpec((buses, rows), lambda i, p: (0, i)),
        ),
        interpret=INTERPRET,
    )(pattern, factors)


def on_device(
    load,
    ptdf,
    ptdf_pattern,
    line_limit,
    unit_bus,
    store_bus,
    tie_block,
    cost_quad,
    cost_lin,
    gen_limit,
    ramp_limit,
    retention,
    store_cap,
    gen_start,
    charge_start,
):
    highest = lax.Precision.HIGHEST
    demand = load[0]
    periods_here, scenarios, buses = demand.shape
    rows = periods_here * scenarios
    lines = ptdf.shape[1]
    stores = charge_start.shape[3]
    network_t = masked_transpose(ptdf_pattern[0], ptdf[0])
    bus_range = jnp.arange(buses, dtype=jnp.int32)
    device_bus = jnp.concatenate([unit_bus[0], store_bus[0]])
    device_map = (device_bus[:, None] == bus_range[None, :]).astype(jnp.bfloat16)
    units = unit_bus.shape[1]
    flow_cap = line_limit[0][None, :]
    ramp_cap = ramp_limit[0]
    quadratic = cost_quad[0]
    linear_cost = cost_lin[0]
    upper = gen_limit[0]
    capacity = store_cap[0]
    keep_rate = retention[0]
    demand_rows = demand.reshape(rows, buses)
    position = lax.axis_index("period")
    nbits = lax.axis_size("region").bit_length() - 1
    at_start = position == 0
    at_end = position == lax.axis_size("period") - 1
    first_here = position * periods_here
    rate_slab = jnp.pad(keep_rate, ((0, scenarios - periods_here), (0, 0)))[None]
    both = gathered(jnp.concatenate([charge_start[0], rate_slab]), "period")
    both = both.reshape(-1, periods_here + 1, scenarios, stores)
    charge_all = both[:, :periods_here].reshape(-1, scenarios, stores)
    rate_all = both[:, periods_here, :periods_here].reshape(-1, stores)
    rate_next = jnp.concatenate([rate_all[1:], jnp.zeros_like(rate_all[:1])])[:, None, :]
    rate_all = rate_all[:, None, :]
    gen = gen_start[0]
    charge = charge_start[0]
    line_dual = jnp.zeros((rows, lines), jnp.float32)
    tie_dual = [jnp.zeros((rows, BLK), jnp.float32) for colour in range(COLORS)]
    ramp_dual = jnp.zeros_like(gen)
    ramp_dual_after = jnp.zeros_like(gen[0])
    store_dual = jnp.zeros_like(charge_all)
    balance_dual = jnp.zeros((rows,), jnp.float32)
    rho = jnp.float32(rho_start)
    for iteration in range(ITERS):
        gen_rows = gen.reshape(rows, -1)
        charge_rows = charge.reshape(rows, stores)
        inject = (
            split_dot(jnp.concatenate([gen_rows, -charge_rows], axis=1), device_map, 0)
            - demand_rows
        )
        flows = jnp.dot(
            inject.astype(jnp.bfloat16), network_t, preferred_element_type=jnp.float32
        )
        over = flows - jnp.clip(flows, -flow_cap, flow_cap)
        line_term = line_dual + rho * over
        flow_term = line_term
        local_primal = jnp.sum(over * over)
        new_ties = []
        for colour in range(COLORS):
            start = tie_block[0, colour] * BLK
            mine = lax.dynamic_slice_in_dim(flows, start, BLK, 1)
            theirs = swapped(mine, "region", colour % nbits)
            mismatch = mine + theirs
            tie_term = tie_dual[colour] + rho * mismatch
            current = lax.dynamic_slice_in_dim(flow_term, start, BLK, 1)
            flow_term = lax.dynamic_update_slice_in_dim(flow_term, current + tie_term, start, 1)
            local_primal = local_primal + jnp.sum(mismatch * mismatch)
            new_ties.append(tie_term)
        grad_inject = lax.dot_general(
            flow_term.astype(jnp.bfloat16),
            network_t,
            (((1,), (1,)), ((), ())),
            preferred_element_type=jnp.float32,
        )
        balance = jnp.mean(inject, axis=1)
        balance_term = balance_dual + rho * balance
        before = passed_along(gen[-1], "period", 1)
        following = passed_along(gen[0], "period", -1)
        earlier = jnp.concatenate([before[None], gen[:-1]], axis=0)
        change = gen - earlier
        ramp_over = change - jnp.clip(change, -ramp_cap, ramp_cap)
        ramp_over = jnp.concatenate(
            [jnp.where(at_start, 0.0, ramp_over[:1]), ramp_over[1:]], axis=0
        )
        ramp_term = ramp_dual + rho * ramp_over
        step_after = following - gen[-1]
        after = ramp_dual_after + rho * (step_after - jnp.clip(step_after, -ramp_cap, ramp_cap))
        after = jnp.where(at_end, 0.0, after)
        ramp_later = jnp.concatenate([ramp_term[1:], after[None]], axis=0)
        soc = recurrence(rate_all, charge_all, False)
        store_over_all = soc - jnp.clip(soc, 0.0, capacity)
        store_term_all = store_dual + rho * store_over_all
        adjoint_all = recurrence(rate_next, store_term_all, True)
        store_over = lax.dynamic_slice_in_dim(store_over_all, first_here, periods_here, 0)
        adjoint = lax.dynamic_slice_in_dim(adjoint_all, first_here, periods_here, 0)
        local_primal = (
            local_primal
            + jnp.sum(ramp_over * ramp_over)
            + jnp.sum(store_over * store_over)
            + jnp.sum(balance * balance)
        )
        push = split_dot(grad_inject, device_map, 1)
        unit_push = push[:, :units].reshape(gen.shape)
        store_push = push[:, units:].reshape(charge.shape)
        balance_wide = balance_term.reshape(periods_here, scenarios, 1)
        grad_gen = quadratic * gen + linear_cost + unit_push + balance_wide + ramp_term - ramp_later
        grad_charge = store_weight * charge + adjoint - store_push - balance_wide
        gen_next = jnp.clip(gen - step_size * grad_gen, 0.0, upper)
        charge_next = jnp.clip(charge - step_size * grad_charge, -0.25 * capacity, 0.25 * capacity)
        gen_step = gen_next - gen
        charge_step = charge_next - charge
        local_change = (jnp.sum(gen_step * gen_step) + jnp.sum(charge_step * charge_step)) / (
            step_size * step_size
        )
        partial = jnp.stack([local_primal, local_change])
        if iteration + 1 < ITERS:
            slab = jnp.pad(partial, (0, stores - 2))
            slab = jnp.broadcast_to(slab, (1, scenarios, stores))
            both = gathered(jnp.concatenate([charge_next, slab]), "period")
            both = both.reshape(-1, periods_here + 1, scenarios, stores)
            charge_all = both[:, :periods_here].reshape(-1, scenarios, stores)
            partial = jnp.sum(both[:, periods_here, 0, :2], axis=0)
            primal, changes = total(partial, ("region",))
        else:
            primal, changes = total(partial, ("region", "period"))
        line_dual = line_term
        tie_dual = new_ties
        ramp_dual = ramp_term
        ramp_dual_after = after
        store_dual = store_term_all
        balance_dual = balance_term
        rho = rho * ((primal + small_eps) / (changes + small_eps)) ** 0.25
        gen = gen_next
        charge = charge_next
    tie_out = jnp.concatenate(tie_dual, axis=1).reshape(periods_here, scenarios, COLORS * BLK)
    return (
        gen[None],
        charge[None],
        line_dual.reshape(periods_here, scenarios, lines)[None],
        tie_out[None],
        rho,
    )


def solution(mesh):
    return jax.shard_map(
        on_device,
        mesh=mesh,
        in_specs=(
            P("region", "period", None, None),
            P("region", None, None),
            P("region", None, None),
            P("region", None),
            P("region", None),
            P("region", None),
            P("region", None),
            P("region", None),
            P("region", None),
            P("region", None),
            P("region", None),
            P("region", "period", None),
            P("region", None),
            P("region", "period", None, None),
            P("region", "period", None, None),
        ),
        out_specs=(
            P("region", "period", None, None),
            P("region", "period", None, None),
            P("region", "period", None, None),
            P("region", "period", None, None),
            P(),
        ),
        check_vma=False,
    )
```
